32 devices in a mesh: dp: 8 (over y, x, core), tensor: 4 (over z).
Axes of the slice: x: 2, y: 2, z: 4, core: 2. Of those that a mesh axis runs over, the one named last changes fastest.
Arguments:
- x_in: bfloat16 [2048, 768], P(('dp', 'tensor')), may hold values from -6 to 6
- segment_ids: int32 [2048], P('dp'), may hold values from 0 to 2, as said below
- norm_gain: float32 [2, 768], replicated, may hold values from 0.1 to 1.9
- w_zx: bfloat16 [2, 768, 2, 1536], P(None, 'dp', None, 'tensor'), may hold values from -0.21875 to 0.21875
- w_dt: bfloat16 [2, 768, 24], P(None, 'dp', 'tensor'), may hold values from -0.21875 to 0.21875
- w_bc: bfloat16 [2, 768, 256], P(None, 'dp'), may hold values from -0.21875 to 0.21875
- conv_x: float32 [2, 4, 1536], P(None, None, 'tensor'), may hold values from -3 to 3
- conv_x_bias: float32 [2, 1536], P(None, 'tensor'), may hold values from -2 to 2
- conv_bc: float32 [2, 4, 256], replicated, may hold values from -3 to 3
- conv_bc_bias: float32 [2, 256], replicated, may hold values from -2 to 2
- dt_bias: float32 [2, 24], P(None, 'tensor'), may hold values from -7 to -2
- a_log: float32 [2, 24], P(None, 'tensor'), may hold values from 0 to 1.5
- d_skip: float32 [2, 24], P(None, 'tensor'), may hold values from 0.5 to 1.5
- gate_gain: float32 [2, 1536], P(None, 'tensor'), may hold values from 0.1 to 1.9
- w_out: bfloat16 [2, 1536, 768], P(None, 'tensor', 'dp'), may hold values from -0.15625 to 0.15625
- cotangent: bfloat16 [2048, 768], P(('dp', 'tensor')), may hold values from -6 to 6
Outputs:
- y_out: bfloat16 [2048, 768], P(('dp', 'tensor'))
- d_x_in: float32 [2048, 768], P(('dp', 'tensor'))
- d_norm_gain: float32 [2, 768], replicated
- d_w_zx: float32 [2, 768, 2, 1536], P(None, 'dp', None, 'tensor')
- d_w_dt: float32 [2, 768, 24], P(None, 'dp', 'tensor')
- d_w_bc: float32 [2, 768, 256], P(None, 'dp')
- d_conv_x: float32 [2, 4, 1536], replicated
- d_conv_x_bias: float32 [2, 1536], replicated
- d_conv_bc: float32 [2, 4, 256], replicated
- d_conv_bc_bias: float32 [2, 256], replicated
- d_dt_bias: float32 [2, 24], replicated
- d_a_log: float32 [2, 24], replicated
- d_d_skip: float32 [2, 24], replicated
- d_gate_gain: float32 [2, 1536], replicated
- d_w_out: float32 [2, 1536, 768], P(None, 'tensor', 'dp')
The draws below stay inside these ranges and needn't reach their ends.
Inputs may be any that keep to these rules, and one draw needn't show every extreme that they name: `segment_ids`: segment numbers start at 0 and rise by one at each new sequence; every sequence but the first and the last has exactly 1024 tokens, the first has 1 to 1023 tokens.
All inputs are finite; a program needn't handle non-finite values.
Results may differ from the reference program's by a relative error of at most 0.012.
The reference program's roundings to bfloat16 on the way count: a program that leaves them out, or rounds other values in their place, can miss the bound.
Values may be sent and summed in bfloat16 or wider, within the bound.
A program may use at most 128 MiB of HBM per device.

```python
import jax
import jax.numpy as jnp
from jax import lax

D = 768
HEADS = 24
HEAD_DIM = 64
STATE = 128
CONV = 4
STRETCH = 256
LAYERS = 2
SEQ_LEN = 1024
INNER = 1536
TOKENS = 2048


def draw_segment_ids(key, part):
    offset = jax.random.randint(key, (), 1, SEQ_LEN)
    places = jnp.arange(TOKENS, dtype=jnp.int32)
    return ((places + offset) // SEQ_LEN).astype(jnp.int32)


def level_of(rng, extent, cuts, smallest, largest):
    def one(position, shards_of):
        steps = jax.random.uniform(jax.random.fold_in(jax.random.fold_in(rng, 6), position), (shards_of,), jnp.float32, smallest / len(cuts), largest / len(cuts))
        return jnp.repeat(jnp.exp(steps), extent[position] // shards_of).reshape((-1,) + (1,) * (len(extent) - position - 1))

    level = one(*cuts[0])
    for cut in cuts[1:]:
        level = level * one(*cut)
    return level


def scatter_about(rng, dims, spread, bound, shards=(), kind=jnp.bfloat16):
    entries = jax.random.normal(rng, dims, jnp.float32) * spread
    if len(shards) > 0:
        entries = level_of(rng, dims, shards, -0.22, 0.18) * entries
    return jnp.clip(entries, min=-bound, max=bound).astype(kind)


def setup_inputs(seed: int = 0) -> dict:
    key_list = jax.random.split(jax.random.key(seed), 17)
    x_in = scatter_about(key_list[0], (TOKENS, D), 1.0, 6.0, ((0, 32),))
    segment_ids = draw_segment_ids(jax.random.fold_in(key_list[16], 71), 0)
    norm_gain = jnp.clip(1.0 + 0.18 * jax.random.normal(key_list[2], (LAYERS, D), jnp.float32), 0.1, 1.9)
    w_zx = scatter_about(key_list[3], (LAYERS, D, 2, INNER), D ** -0.5, 0.21875, ((1, 8), (3, 4)))
    w_dt = scatter_about(key_list[4], (LAYERS, D, HEADS), D ** -0.5, 0.21875, ((1, 8), (2, 4)))
    w_bc = scatter_about(key_list[5], (LAYERS, D, 2 * STATE), D ** -0.5, 0.21875, ((1, 8),))
    conv_x = scatter_about(key_list[6], (LAYERS, CONV, INNER), 0.5, 3.0, ((2, 4),), jnp.float32)
    conv_x_bias = scatter_about(key_list[7], (LAYERS, INNER), 0.3, 2.0, ((1, 4),), jnp.float32)
    conv_bc = scatter_about(key_list[8], (LAYERS, CONV, 2 * STATE), 0.5, 3.0, (), jnp.float32)
    conv_bc_bias = scatter_about(key_list[9], (LAYERS, 2 * STATE), 0.3, 2.0, (), jnp.float32)
    dt_bias = jnp.clip(-7.0 + 5.0 * jax.random.uniform(key_list[10], (LAYERS, HEADS), jnp.float32) ** level_of(key_list[10], (LAYERS, HEADS), ((1, 4),), -0.2, 0.2), -7.0, -2.0)
    a_log = jnp.clip(1.5 * jax.random.uniform(key_list[11], (LAYERS, HEADS), jnp.float32) ** level_of(key_list[11], (LAYERS, HEADS), ((1, 4),), -0.2, 0.2), 0.0, 1.5)
    d_skip = jnp.clip(0.5 + 1.0 * jax.random.uniform(key_list[12], (LAYERS, HEADS), jnp.float32) ** level_of(key_list[12], (LAYERS, HEADS), ((1, 4),), -0.2, 0.2), 0.5, 1.5)
    gate_gain = jnp.clip(1.0 + 0.18 * jax.random.normal(key_list[13], (LAYERS, INNER), jnp.float32), 0.1, 1.9)
    w_out = scatter_about(key_list[14], (LAYERS, INNER, D), INNER ** -0.5, 0.15625, ((1, 4), (2, 8)))
    cotangent = scatter_about(key_list[15], (TOKENS, D), 1.0, 6.0, ((0, 32),))
    return dict(x_in=x_in, segment_ids=segment_ids, norm_gain=norm_gain, w_zx=w_zx, w_dt=w_dt, w_bc=w_bc, conv_x=conv_x, conv_x_bias=conv_x_bias, conv_bc=conv_bc, conv_bc_bias=conv_bc_bias, dt_bias=dt_bias, a_log=a_log, d_skip=d_skip, gate_gain=gate_gain, w_out=w_out, cotangent=cotangent)


EPSILON = 1e-05
PRECISE = lax.Precision.HIGHEST

@jax.custom_vjp
def low(v):
    return lax.optimization_barrier(v.astype(jnp.bfloat16)).astype(jnp.float32)

@jax.custom_vjp
def low_back(v):
    return v

def low_keep(v):
    return (low(v), None)

def low_pass(kept, grad):
    return (grad,)

def back_keep(v):
    return (v, None)

def back_low(kept, grad):
    return (low(grad),)
low.defvjp(low_keep, low_pass)
low_back.defvjp(back_keep, back_low)

def stretch_core(xs_block, b_block, c_block, dt_block, la_block, skip_gain, seg_block, seg_before, state_in):
    cumulative = jnp.cumsum(la_block, axis=0)
    length = seg_block.shape[0]
    places = jnp.arange(length)
    inside = (seg_block[:, None] == seg_block[None, :]) & (places[:, None] >= places[None, :])
    span_logs = cumulative[:, None, :] - cumulative[None, :, :]
    decays = jnp.exp(jnp.where(inside[:, :, None], span_logs, -1e+30))
    scores = jnp.dot(c_block, b_block.T, precision=PRECISE)
    scaled = xs_block * dt_block[:, :, None]
    output = jnp.einsum('ijh,ij,jhp->ihp', decays, scores, scaled, precision=PRECISE)
    reached = (seg_block == seg_before).astype(jnp.float32)
    carried = jnp.einsum('in,hpn->ihp', c_block, state_in, precision=PRECISE)
    output = output + jnp.exp(cumulative)[:, :, None] * reached[:, None, None] * carried
    output = output + skip_gain[None, :, None] * xs_block
    last_seg = seg_block[length - 1]
    kept_rows = (seg_block == last_seg).astype(jnp.float32)
    to_end = jnp.exp(cumulative[length - 1][None, :] - cumulative) * kept_rows[:, None]
    whole_seg = (last_seg == seg_before).astype(jnp.float32)
    new_state = (whole_seg * jnp.exp(cumulative[length - 1]))[:, None, None] * state_in
    new_state = new_state + jnp.einsum('jh,jhp,jn->hpn', to_end, scaled, b_block, precision=PRECISE)
    return (output, new_state)

def conv_apply(extended, seg_extended, segments, conv_weight, conv_bias):
    length = segments.shape[0]
    tap_count = conv_weight.shape[0]
    result = jnp.zeros((length, extended.shape[1]), jnp.float32) + conv_bias
    for tap_index in range(tap_count):
        same_seg = (seg_extended[tap_index:tap_index + length] == segments).astype(jnp.float32)
        result = result + conv_weight[tap_index] * extended[tap_index:tap_index + length] * same_seg[:, None]
    return result

def run_layer(hidden, seg_blocks, seg_windows, seg_before, params):
    gain, w_zpart, w_xpart, w_dtpart, w_bcpart, conv_weight, conv_bias, bias_dt, log_rate, skip_gain, gate_weight, w_outpart = params
    margin = CONV - 1

    def advance(carry, pieces):
        tail_rows, state_in = carry
        rows_in, seg_block, seg_window, before_seg = pieces
        rms_scale = lax.rsqrt(lax.optimization_barrier(jnp.mean(rows_in * rows_in, axis=1, keepdims=True)) + EPSILON)
        normed = low(rows_in * rms_scale * gain)
        proj_z = low_back(jnp.dot(normed, w_zpart, precision=PRECISE))
        proj_x = low(low_back(jnp.dot(normed, w_xpart, precision=PRECISE)))
        proj_dt = low_back(jnp.dot(normed, w_dtpart, precision=PRECISE))
        proj_bc = low(jnp.dot(normed, w_bcpart, precision=PRECISE))
        conv_in = jnp.concatenate([proj_x, proj_bc], axis=1)
        extended = jnp.concatenate([tail_rows, conv_in], axis=0)
        activated = jax.nn.silu(conv_apply(extended, seg_window, seg_block, conv_weight, conv_bias))
        xs_heads = activated[:, :INNER].reshape(STRETCH, HEADS, HEAD_DIM)
        b_mat = activated[:, INNER:INNER + STATE]
        c_mat = activated[:, INNER + STATE:]
        step_dt = jax.nn.softplus(proj_dt + bias_dt)
        log_decay = -step_dt * jnp.exp(log_rate)
        heads_y, state_out = stretch_core(xs_heads, b_mat, c_mat, step_dt, log_decay, skip_gain, seg_block, before_seg, state_in)
        gated_y = heads_y.reshape(STRETCH, INNER) * jax.nn.silu(proj_z)
        mixed_out = low(gated_y * lax.rsqrt(lax.optimization_barrier(jnp.mean(gated_y * gated_y, axis=1, keepdims=True)) + EPSILON) * gate_weight)
        branch = low_back(jnp.dot(mixed_out, w_outpart, precision=PRECISE))
        return ((extended[STRETCH:], state_out), rows_in + branch)
    start_carry = (jnp.zeros((margin, INNER + 2 * STATE), jnp.float32), jnp.zeros((HEADS, HEAD_DIM, STATE), jnp.float32))
    block_count = hidden.shape[0] // STRETCH
    finals, outputs = lax.scan(jax.checkpoint(advance), start_carry, (hidden.reshape(block_count, STRETCH, D), seg_blocks, seg_windows, seg_before))
    return outputs.reshape(hidden.shape[0], D)

def reference(x_in, segment_ids, norm_gain, w_zx, w_dt, w_bc, conv_x, conv_x_bias, conv_bc, conv_bc_bias, dt_bias, a_log, d_skip, gate_gain, w_out, cotangent):
    token_count = x_in.shape[0]
    block_count = token_count // STRETCH
    margin = CONV - 1
    padded = jnp.concatenate([jnp.full((margin,), -1, jnp.int32), segment_ids.astype(jnp.int32)])
    window_index = (jnp.arange(block_count, dtype=jnp.int32)[:, None] * STRETCH + jnp.arange(STRETCH + margin, dtype=jnp.int32)[None, :]).astype(jnp.int32)
    seg_windows = padded[window_index]
    seg_blocks = segment_ids.astype(jnp.int32).reshape(block_count, STRETCH)
    seg_before = seg_windows[:, margin - 1]

    def forward(hidden, gain_all, zx_all, dt_all, bc_all, convx_all, convxb_all, convbc_all, convbcb_all, dtb_all, alog_all, skip_all, gate_all, out_all):
        for layer_num in range(LAYERS):
            params = (gain_all[layer_num], zx_all[layer_num][:, 0, :], zx_all[layer_num][:, 1, :], dt_all[layer_num], bc_all[layer_num], jnp.concatenate([convx_all[layer_num], convbc_all[layer_num]], axis=1), jnp.concatenate([convxb_all[layer_num], convbcb_all[layer_num]]), dtb_all[layer_num], alog_all[layer_num], skip_all[layer_num], gate_all[layer_num], out_all[layer_num])
            hidden = run_layer(hidden, seg_blocks, seg_windows, seg_before, params)
        return hidden
    result, pullback = jax.vjp(forward, x_in.astype(jnp.float32), norm_gain.astype(jnp.float32), w_zx.astype(jnp.float32), w_dt.astype(jnp.float32), w_bc.astype(jnp.float32), conv_x.astype(jnp.float32), conv_x_bias.astype(jnp.float32), conv_bc.astype(jnp.float32), conv_bc_bias.astype(jnp.float32), dt_bias.astype(jnp.float32), a_log.astype(jnp.float32), d_skip.astype(jnp.float32), gate_gain.astype(jnp.float32), w_out.astype(jnp.float32))
    grads = pullback(cotangent.astype(jnp.float32))
    return (result.astype(jnp.bfloat16), grads[0], grads[1], grads[2], grads[3], grads[4], grads[5], grads[6], grads[7], grads[8], grads[9], grads[10], grads[11], grads[12], grads[13])
```

```python
import types

import jax
import jax.numpy as jnp
from jax import lax
from jax.experimental import pallas as pl
from jax.experimental.pallas import tpu as pltpu
from jax.sharding import PartitionSpec as P

EPSILON = 1e-05
MESH = pl.DeviceIdType.MESH
DP, TP = "dp", "tensor"
F32 = jnp.float32
BF16 = jnp.bfloat16
HALO = 16
LANES = 128


def pieces(value, count):
    found = []
    for _ in range(count):
        high = value.astype(BF16)
        found.append(high)
        value = value - high.astype(F32)
    return found


def dot(a, b, over_a=1, over_b=0):
    return lax.dot_general(
        a, b, (((over_a,), (over_b,)), ((), ())), preferred_element_type=F32
    )


def fine_dot(a, exact, over_a=1, over_b=0, count=3):
    return sum(dot(part, exact, over_a, over_b) for part in pieces(a, count))


def wide(value, times):
    return jnp.concatenate([value] * times, axis=1)


def sigmoid(v):
    return 1.0 / (1.0 + jnp.exp(-v))


class Links:
    def __init__(self, send, recv):
        self.send, self.recv, self.used = send, recv, 0

    def take(self, count=1):
        self.used += count
        return self.used - count

    def copy(self, src, dst, device, send_at, recv_at):
        return pltpu.make_async_remote_copy(
            src_ref=src,
            dst_ref=dst,
            send_sem=self.send.at[send_at],
            recv_sem=self.recv.at[recv_at],
            device_id=device,
            device_id_type=MESH,
        )


def whole_step(sizes, refs):
    layers, T, D, inner, conv_width, dc, tc, gather_weights, state_width = sizes
    R = T // tc
    ext_rows = T + HALO
    bc_at = 2 * inner
    dt_at = inner + conv_width
    out_at = dt_at + LANES
    columns = out_at + inner
    full_inner = inner * tc
    head_width = refs.head_width
    per = LANES // head_width
    chunks = inner // LANES
    depth = D // dc
    lx = Links(refs.send, refs.recv)
    a, t = lax.axis_index(DP), lax.axis_index(TP)
    last_t = tc - 1
    prev, following = lax.rem(a + dc - 1, dc), lax.rem(a + 1, dc)
    half = dc // 2
    core = lax.rem(a, 2)
    sibling = a + 1 - 2 * core

    barrier = pltpu.get_barrier_semaphore()
    greeted = 0
    for s in range(1, tc):
        pl.semaphore_signal(
            barrier, inc=1, device_id={DP: a, TP: lax.rem(t + s, tc)}, device_id_type=MESH
        )
        greeted += 1
    for s in range(1, dc):
        near = s == 1 or s == dc - 1
        for u in range(tc if near else 1):
            pl.semaphore_signal(
                barrier,
                inc=1,
                device_id={DP: lax.rem(a + s, dc), TP: lax.rem(t + u, tc)},
                device_id_type=MESH,
            )
            greeted += 1

    lane = lax.broadcasted_iota(jnp.int32, (1, LANES), 1)
    low_half = lane < head_width
    spread = refs.spread
    rows_i = lax.broadcasted_iota(jnp.int32, (LANES, inner), 0)
    cols_i = lax.broadcasted_iota(jnp.int32, (LANES, inner), 1)
    spread[...] = (
        (cols_i >= rows_i * head_width) & (cols_i < (rows_i + 1) * head_width)
    ).astype(F32).astype(BF16)
    below = refs.below
    tri_i = lax.broadcasted_iota(jnp.int32, (T, T), 0)
    tri_j = lax.broadcasted_iota(jnp.int32, (T, T), 1)
    below[...] = (tri_i >= tri_j).astype(F32).astype(BF16)
    seg_ext, masks, bias = refs.seg_ext, refs.masks, refs.bias
    seg_ext[HALO:, :] = refs.seg_col[...]
    seg_col = refs.seg_col[...]
    inside = (wide(seg_col, T // LANES) == refs.seg_row[0:1, :]) & (tri_i >= tri_j)
    bias[...] = jnp.where(inside, 0.0, -1e30)

    def own_rows(ref, offset=0):
        return ref.at[pl.ds(pl.multiple_of(offset + t * R, 16), R)]

    def start_rows(ref, offset, halo):
        base = lx.take(tc + (2 * tc if halo else 0))
        sent = []
        if halo:
            for u in range(tc):
                c = lx.copy(
                    ref.at[pl.ds(T, HALO)],
                    ref.at[pl.ds(0, HALO)],
                    {DP: following, TP: jnp.int32(u)},
                    base + tc + u,
                    base + tc,
                )
                pl.when(t == last_t)(c.start)
        for s in range(1, tc):
            c = lx.copy(
                own_rows(ref, offset),
                own_rows(ref, offset),
                {DP: a, TP: lax.rem(t + s, tc)},
                base + s,
                base + s,
            )
            c.start()
            sent.append(c)

        def finish():
            for c in sent:
                c.wait()
            if halo:
                for u in range(tc):
                    c = lx.copy(
                        ref.at[pl.ds(T, HALO)],
                        ref.at[pl.ds(0, HALO)],
                        {DP: following, TP: jnp.int32(u)},
                        base + tc + u,
                        base + tc,
                    )
                    pl.when(t == last_t)(c.wait_send)
                c.wait_recv()

        return finish

    def start_blocks(ref, axis):
        count, me = (dc, a) if axis == DP else (tc, t)
        base = lx.take(count)
        sent = []
        for s in range(1, count):
            c = lx.copy(
                ref.at[me],
                ref.at[me],
                {DP: a, TP: t, axis: lax.rem(me + s, count)},
                base + s,
                base + s,
            )
            c.start()
            sent.append(c)

        def finish():
            for c in sent:
                c.wait()

        return finish

    def start_shared(view):
        base = lx.take(dc)
        own = lx.copy(view(a), view(a), {DP: sibling, TP: t}, base, base)
        across = []
        for s in range(1, half):
            peer = lax.rem(a + 2 * s, dc)
            c = lx.copy(view(a), view(a), {DP: peer, TP: t}, base + s, base + s)
            c.start()
            across.append(c)
        own.start()

        def finish():
            passed = []
            for s in range(1, half):
                across[s - 1].wait_recv()
                source = lax.rem(a + dc - 2 * s, dc)
                c = lx.copy(
                    view(source), view(source), {DP: sibling, TP: t}, base + half + s, base + half + s
                )
                c.start()
                passed.append(c)
            own.wait()
            for c in across:
                c.wait_send()
            for c in passed:
                c.wait()

        return finish

    def start_pairs(source, pairs, got):
        base = lx.take(dc)
        sent = []
        for k in range(half):
            c = lx.copy(
                source.at[depth_block(2 * k + 1 - core)],
                pairs.at[k],
                {DP: sibling, TP: t},
                base + k,
                base + k,
            )
            c.start()
            sent.append(c)

        def second():
            for c in sent:
                c.wait()
            across = []
            for s in range(1, half + 1):
                peer = lax.rem(a + 2 * s, dc)
                k = peer // 2
                total = source[depth_block(peer), :].astype(F32) + pairs[k].astype(F32)
                if s == half:
                    got[a // 2] = total.astype(BF16)
                    continue
                pairs[k] = total.astype(BF16)
                c = lx.copy(
                    pairs.at[k],
                    got.at[a // 2],
                    {DP: peer, TP: t},
                    base + half + s,
                    base + half + s,
                )
                c.start()
                across.append(c)

            def finish():
                for c in across:
                    c.wait()

            return finish

        return second

    def start_owners(source, block_of, ref, axis):
        count, me = (dc, a) if axis == DP else (tc, t)
        base = lx.take(count)
        sent = []
        for s in range(1, count):
            peer = lax.rem(me + s, count)
            c = lx.copy(
                source.at[block_of(peer)],
                ref.at[me],
                {DP: a, TP: t, axis: peer},
                base + s,
                base + s,
            )
            c.start()
            sent.append(c)
        ref[me] = source[block_of(me)]

        def finish():
            for c in sent:
                c.wait()

        return finish

    def token_block(offset):
        return lambda peer: pl.ds(pl.multiple_of(offset + peer * R, 16), R)

    def depth_block(peer):
        return pl.ds(pl.multiple_of(peer * depth, 16), depth)

    def start_weights(l):
        ref = refs.weights.at[l]
        ref[depth_block(a), :] = refs.packed[l]
        return start_shared(lambda i: ref.at[depth_block(i)])

    own_x = own_rows(refs.x_all, HALO)
    own_x[...] = refs.x_in[...]
    own_c = own_rows(refs.cot_all)
    own_c[...] = refs.cotangent[...]

    pl.semaphore_wait(barrier, greeted)

    seg_base = lx.take()
    seg_copy = lx.copy(
        refs.seg_col.at[pl.ds(T - HALO, HALO)],
        seg_ext.at[pl.ds(0, HALO)],
        {DP: following, TP: t},
        seg_base,
        seg_base,
    )
    seg_copy.start()
    rows_done = start_rows(refs.x_all, HALO, True)
    weights_done = start_weights(0) if gather_weights else lambda: None
    seg_copy.wait()
    seg_ext[0:HALO, :] = jnp.where(a == 0, -1.0, seg_ext[0:HALO, :])
    for k in range(3):
        masks[k] = (seg_ext[pl.ds(HALO - 3 + k, T), :] == seg_col).astype(F32)
    first_seg, last_seg = seg_ext[HALO : HALO + 1, :], seg_ext[ext_rows - 1 :, :]
    reached = (seg_col == first_seg).astype(F32)
    kept = (seg_col == last_seg).astype(F32)
    joined = wide((seg_ext[HALO - 1 : HALO, :] == first_seg).astype(F32), chunks)
    whole_seg = wide((last_seg == first_seg).astype(F32), chunks)
    refs.reached[...] = reached
    refs.kept[...] = kept
    rows_done()

    def row(l, at, width):
        return refs.params[l, at : at + 1, :width]

    def norm_rows(h, gain):
        scale = lax.rsqrt(jnp.mean(h * h, axis=1, keepdims=True) + EPSILON)
        return (h * scale * gain).astype(BF16)

    refs.normed[0] = norm_rows(refs.x_all[...].astype(F32), row(0, 6, D))
    refs.hidden[0] = own_x[...].astype(F32)

    def as_column(value):
        return fine_dot(value, jnp.full((8, LANES), 0.125, BF16), 0, 0)

    def row_sums(value):
        return fine_dot_rows(value)

    def fine_dot_rows(value):
        ones = jnp.ones((8, inner), BF16)
        return sum(dot(ones, part, 1, 1) for part in pieces(value, 2))

    def forward(l):
        W = refs.weights.at[l]
        nx, ext, pre, act = (r.at[l] for r in (refs.normed, refs.ext, refs.pre, refs.act))
        tokens = pl.ds(HALO, T)
        refs.z[l] = dot(nx[tokens, :], W[:, :inner])
        ext[...] = dot(nx[...], W[:, inner:dt_at]).astype(BF16).astype(F32)
        dtb = dot(nx[tokens, :], W[:, dt_at:out_at]) + row(l, 7, LANES)
        for c in range(conv_width // LANES):
            at = slice(c * LANES, (c + 1) * LANES)
            taps = refs.params[l, 0:5, at]
            total = taps[4:5] + taps[3:4] * ext[tokens, at]
            for k in range(3):
                total = total + taps[k : k + 1] * ext[pl.ds(HALO - 3 + k, T), at] * masks[k]
            pre[:, at] = total
            act[:, at] = total * sigmoid(total)
        step = jnp.maximum(dtb, 0.0) + jnp.log1p(jnp.exp(-jnp.abs(dtb)))
        decay = -step * jnp.exp(row(l, 8, LANES))
        cum = sum(dot(below[...], part) for part in pieces(decay, 3))
        refs.dtb[l] = dtb
        refs.decay[l] = decay
        step_wide = fine_dot(step, spread[...])
        cum_wide = fine_dot(cum, spread[...])
        end = cum_wide[T - 1 :, :]
        from_start = jnp.exp(cum_wide) * wide(refs.reached[...], chunks)
        to_end = jnp.exp(end - cum_wide) * wide(refs.kept[...], chunks)
        refs.step_wide[l] = step_wide
        refs.from_start[l] = from_start
        refs.to_end[l] = to_end
        end_decay = jnp.exp(end)
        refs.end_decay[l] = end_decay
        xs = act[:, :inner]
        scaled = xs * step_wide
        refs.scaled[l] = scaled.astype(BF16)
        bmat = act[:, inner : inner + state_width].astype(BF16)
        cmat = act[:, inner + state_width :].astype(BF16)
        refs.bmat[l] = bmat
        refs.cmat[l] = cmat
        states, coefs = refs.states.at[l], refs.coefs.at[l]
        states[a, :state_width] = dot(bmat, (scaled * to_end).astype(BF16), 0, 0).astype(BF16)
        parts = pieces(joined * whole_seg * end_decay, 3)
        states[a, state_width:] = jnp.concatenate(
            parts + [jnp.zeros((13, inner), BF16)], axis=0
        )
        states_done = start_shared(lambda i: states.at[i])
        scores = dot(cmat, bmat, 1, 1)
        refs.scores[l] = scores
        cum_rows = cum.T
        for c in range(chunks):
            at = slice(c * LANES, (c + 1) * LANES)
            pair = refs.scaled[l, :, at]
            found = []
            for u in range(per):
                h = c * per + u
                span = cum[:, h : h + 1] - cum_rows[h : h + 1, :] + bias[...]
                kernel_h = jnp.exp(span)
                refs.spans[l, h] = kernel_h
                mixed_h = (kernel_h * scores).astype(BF16)
                refs.mixing[l, h] = mixed_h
                found.append(dot(mixed_h, pair))
            refs.ssd[l, :, at] = choose(found) + row(l, 9, inner)[:, at] * act[:, at]
        states_done()

        def keep(s, carry):
            coefs[s] = jnp.broadcast_to(
                jnp.sum(states[s, state_width:].astype(F32), axis=0, keepdims=True), (8, inner)
            )
            return carry

        lax.fori_loop(0, dc, keep, 0)
        return states, coefs

    def choose(found):
        result = found[0]
        for u in range(1, per):
            result = jnp.where(lane < u * head_width, result, found[u])
        return result

    def enter(values, coefs, backward):
        def step(i, state):
            s = dc - 1 - i if backward else i
            ahead = s > a if backward else s < a
            later = values[s, :state_width].astype(F32) + coefs[s][0:1, :] * state
            return jnp.where(ahead, later, state)

        return lax.fori_loop(0, dc, step, jnp.zeros((state_width, inner), F32))

    def gate(l, states, coefs):
        start = joined * enter(states, coefs, False)
        refs.start[l] = start
        refs.ssd[l] = refs.ssd[l] + refs.from_start[l] * dot(
            refs.cmat[l], start.astype(BF16)
        )
        z = refs.z[l]
        return refs.ssd[l] * (z * sigmoid(z))

    def project_out(l, gated):
        W = refs.weights.at[l]
        unscaled = (gated * row(l, 5, inner)).astype(BF16)
        refs.partial[l] = dot(unscaled, W[:, out_at:], 1, 1).astype(BF16)
        return start_owners(refs.partial.at[l], token_block(0), refs.landed.at[l], TP)

    def summed(ref, count):
        total = ref[0].astype(F32)
        for s in range(1, count):
            total = total + ref[s].astype(F32)
        return total

    def inverse_from(l):
        squares = summed(refs.tokens.at[l], tc)
        inverse = lax.rsqrt(squares[0:8] / full_inner + EPSILON)
        refs.inverse[l] = as_column(inverse)
        return squares

    own_tokens = pl.ds(pl.multiple_of(t * R, 16), R)

    weights_done()
    states, coefs = forward(0)
    weights_done = start_weights(1) if gather_weights else lambda: None
    cot_done = start_rows(refs.cot_all, 0, False)
    gated = gate(0, states, coefs)
    refs.tokens[0, t] = jnp.concatenate([fine_dot_rows(gated * gated)] * 2, axis=0)
    squares_done = start_blocks(refs.tokens.at[0], TP)
    branch_done = project_out(0, gated)
    squares_done()
    inverse_from(0)
    branch_done()
    branch = summed(refs.landed.at[0], tc)
    refs.unscaled[...] = branch
    h1 = refs.hidden[0] + wide(refs.inverse[0, own_tokens, :], D // LANES) * branch
    refs.hidden[1] = h1
    own_n = own_rows(refs.normed.at[1], HALO)
    own_n[...] = norm_rows(h1, row(1, 6, D))
    rows_done = start_rows(refs.normed.at[1], HALO, True)
    cot_done()
    weights_done()
    rows_done()
    states, coefs = forward(1)
    W1 = refs.weights.at[1]
    d_mixed = dot(refs.cot_all[...], W1[:, out_at:])
    gated = gate(1, states, coefs)
    refs.tokens[1, t] = jnp.concatenate(
        [fine_dot_rows(gated * gated), fine_dot_rows(d_mixed * gated * row(1, 5, inner))], axis=0
    )
    squares_done = start_blocks(refs.tokens.at[1], TP)
    out_done = project_out(1, gated)
    squares_done()
    totals = inverse_from(1)
    inner_dot = as_column(totals[8:16])

    def head_sums(value, count=2):
        return sum(dot(part, spread[...], 1, 1) for part in pieces(value, count))

    def put_small(l, at, value, lane_at=0):
        refs.small[l, at : at + value.shape[0], lane_at : lane_at + value.shape[1]] = value

    def column_sum(value):
        return jnp.sum(value, axis=0, keepdims=True)

    def backward(l, grad_rows, d_mixed, inner_dot):
        W = refs.weights.at[l]
        nx, ext, pre, act = (r.at[l] for r in (refs.normed, refs.ext, refs.pre, refs.act))
        d_all, d_low = refs.d_all, refs.d_low
        z, ssd = refs.z[l], refs.ssd[l]
        sig = sigmoid(z)
        silu = z * sig
        gated = ssd * silu
        inverse = wide(refs.inverse[l], chunks)
        gain = row(l, 5, inner)
        scaled_gate = gated * inverse
        mixed = (scaled_gate * gain).astype(BF16)
        put_small(l, 5, column_sum(d_mixed * scaled_gate))
        d_gated = inverse * gain * d_mixed - scaled_gate * inverse * inverse * (
            wide(inner_dot, chunks) / full_inner
        )
        tokens = pl.ds(HALO, T)
        d_all[0:HALO, 0:inner] = jnp.zeros((HALO, inner), BF16)
        d_all[0:HALO, dt_at:out_at] = jnp.zeros((HALO, LANES), BF16)
        d_all[tokens, 0:inner] = (d_gated * ssd * sig * (1.0 + z * (1.0 - sig))).astype(BF16)
        d_ssd = d_gated * silu
        d_ssd_low = d_ssd.astype(BF16)
        refs.d_ssd[...] = d_ssd_low
        from_start = (d_ssd * refs.from_start[l]).astype(BF16)
        d_states = refs.states.at[layers - 1 - l]
        cmat, bmat = refs.cmat[l], refs.bmat[l]
        d_states[a, :state_width] = (joined * dot(cmat, from_start, 0, 0)).astype(BF16)
        d_states_done = start_shared(lambda i: d_states.at[i, pl.ds(0, state_width)])
        start = refs.start[l]
        d_scores = jnp.zeros((T, T), F32)
        for c in range(chunks):
            at = slice(c * LANES, (c + 1) * LANES)
            pair, d_pair = refs.scaled[l, :, at], refs.d_ssd[:, at]
            found = []
            for u in range(per):
                h = c * per + u
                here = (lane >= u * head_width) & (lane < (u + 1) * head_width)
                d_mixing = dot(jnp.where(here, d_pair, jnp.zeros_like(d_pair)), pair, 1, 1)
                d_scores = d_scores + d_mixing * refs.spans[l, h]
                found.append(dot(refs.mixing[l, h], d_pair, 0, 0))
            refs.d_scaled[:, at] = choose(found)
        d_scores = d_scores.astype(BF16)
        d_cmat = dot(d_scores, bmat) + dot(from_start, start.astype(BF16), 1, 1)
        d_bmat = dot(d_scores, cmat, 0, 0)
        d_first, d_second = refs.d_first.at[l], refs.d_second.at[l]
        d_first[:, :inner] = dot(nx[...], d_all[:, :inner], 0, 0).astype(BF16)
        d_first[:, inner:] = dot(grad_rows, mixed, 0, 0).astype(BF16)
        d_states_done()
        if gather_weights:
            second = start_pairs(d_first, refs.pairs.at[l, 0], refs.got.at[l, 0])
        d_end = enter(d_states, refs.coefs.at[l], True)
        d_end_low = d_end.astype(BF16)
        to_end = refs.to_end[l]
        scaled_low = refs.scaled[l].astype(F32)
        from_end = to_end * dot(bmat, d_end_low)
        d_scaled = refs.d_scaled[...] + from_end
        d_bmat = d_bmat + dot((scaled_low * to_end).astype(BF16), d_end_low, 1, 1)
        xs = act[:, :inner]
        skip = row(l, 9, inner)
        d_cum = d_ssd_low.astype(F32) * (ssd - skip * xs) - scaled_low * d_scaled
        d_last = column_sum(scaled_low * from_end) + whole_seg * refs.end_decay[
            l
        ] * column_sum(d_end * start)
        is_last = lax.broadcasted_iota(jnp.int32, (T, inner), 0) == T - 1
        d_cum = head_sums(d_cum + jnp.where(is_last, d_last, 0.0), 3)
        d_decay = sum(dot(below[...], part, 0, 0) for part in pieces(d_cum, 3))
        d_step = head_sums(xs * d_scaled) - d_decay * jnp.exp(row(l, 8, LANES))
        d_dt = d_step * sigmoid(refs.dtb[l])
        d_all[tokens, dt_at:out_at] = d_dt.astype(BF16)
        put_small(l, 0, column_sum(d_dt), conv_width)
        put_small(l, 1, column_sum(d_decay * refs.decay[l]), conv_width)
        put_small(l, 2, head_sums(jnp.broadcast_to(column_sum(xs * d_ssd), (8, inner)))[0:1], conv_width)
        d_xs = refs.step_wide[l] * d_scaled + skip * d_ssd
        for c in range(conv_width // LANES):
            at = slice(c * LANES, (c + 1) * LANES)
            if c < chunks:
                d_act = d_xs[:, at]
            else:
                both = jnp.concatenate([d_bmat, d_cmat], axis=1)
                d_act = both[:, (c - chunks) * LANES : (c - chunks + 1) * LANES]
            p = pre[:, at]
            s = sigmoid(p)
            d_pre = d_act * s * (1.0 + p * (1.0 - s))
            taps = refs.params[l, 0:5, at]
            top = jnp.zeros((HALO, LANES), F32)
            put_small(l, 4, column_sum(d_pre), c * LANES)
            put_small(l, 3, column_sum(d_pre * ext[tokens, at]), c * LANES)
            d_ext = jnp.concatenate([top, d_pre * taps[3:4]], axis=0)
            for k in range(3):
                part = d_pre * masks[k]
                put_small(
                    l, k, column_sum(part * ext[pl.ds(HALO - 3 + k, T), at]), c * LANES
                )
                moved = jnp.concatenate([top, part * taps[k : k + 1]], axis=0)
                d_ext = d_ext + pltpu.roll(moved, ext_rows - 3 + k, 0)
            at_all = slice(inner + c * LANES, inner + (c + 1) * LANES)
            high = d_ext.astype(BF16)
            d_all[:, at_all] = high
            if c >= chunks:
                d_low[:, (c - chunks) * LANES : (c - chunks + 1) * LANES] = (
                    d_ext - high.astype(F32)
                ).astype(BF16)
        rows = dot(d_all[...], W[:, :out_at], 1, 1) + dot(d_low[...], W[:, bc_at:dt_at], 1, 1)
        refs.d_rows[l] = rows.astype(BF16)
        done = start_owners(
            refs.d_rows.at[l], token_block(HALO), refs.d_landed.at[l], TP
        )
        base = lx.take(tc + 1)

        def head_copy():
            return lx.copy(
                refs.d_rows.at[l].at[pl.ds(0, HALO)],
                refs.d_heads.at[l].at[t],
                {DP: prev, TP: jnp.int32(last_t)},
                base + tc,
                base + t,
            )

        head_copy().start()

        if gather_weights:
            first_done = second()
        maps_at, steps_at = bc_at - inner, dt_at - inner
        d_second[:, :maps_at] = dot(nx[...], d_all[:, inner:bc_at], 0, 0).astype(BF16)
        d_second[:, maps_at:steps_at] = (
            dot(nx[...], d_all[:, bc_at:dt_at], 0, 0) + dot(nx[...], d_low[...], 0, 0)
        ).astype(BF16)
        d_second[:, steps_at:] = dot(nx[...], d_all[:, dt_at:out_at], 0, 0).astype(BF16)
        if gather_weights:
            second = start_pairs(d_second, refs.pairs.at[l, 1], refs.got.at[l, 1])
            second_done = second()

        def gradients():
            if gather_weights:
                first_done()
                second_done()

        def finish():
            done()
            head_copy().wait_send()

            @pl.when(t == last_t)
            def _():
                for u in range(tc):
                    lx.copy(
                        refs.d_rows.at[l].at[pl.ds(0, HALO)],
                        refs.d_heads.at[l].at[u],
                        {DP: prev, TP: jnp.int32(last_t)},
                        base + tc,
                        base + u,
                    ).wait_recv()

            refs.d_own[...] = summed(refs.d_landed.at[l], tc)

            @pl.when(t == last_t)
            def _():
                refs.d_own[R - HALO :, :] = refs.d_own[R - HALO :, :] + summed(
                    refs.d_heads.at[l], tc
                )

        return finish, gradients

    def norm_back(l, grad):
        h, d = refs.hidden[l], refs.d_own[...]
        scale = lax.rsqrt(jnp.mean(h * h, axis=1, keepdims=True) + EPSILON)
        put_small(l, 6, column_sum(d * h * scale))
        weighted = d * row(l, 6, D)
        return (
            grad
            + scale * weighted
            - h * scale * scale * scale * jnp.mean(weighted * h, axis=1, keepdims=True)
        )

    for l in range(layers):
        refs.small[l] = jnp.zeros_like(refs.small[l])

    def start_small(l):
        refs.small_all[l, a] = refs.small[l]
        return start_blocks(refs.small_all.at[l], DP)

    finish, gradients1 = backward(1, refs.cot_all[...], d_mixed, inner_dot)
    finish()
    grad = norm_back(1, own_c[...].astype(F32))
    refs.grad[...] = grad
    grads_all = refs.grads_all
    low = grad.astype(BF16)
    here = own_rows(grads_all)
    here[:, :D] = low
    dots = jnp.sum(low.astype(F32) * refs.unscaled[...], axis=1, keepdims=True)
    high, mid, rest = pieces(jnp.broadcast_to(dots, (R, LANES)), 3)
    zero = jnp.zeros_like(high)
    here[:, D:] = jnp.where(
        lane == 0, high, jnp.where(lane == 1, mid, jnp.where(lane == 2, rest, zero))
    )
    grads_done = start_rows(grads_all, 0, False)
    small1 = start_small(1)
    out_done()
    refs.y_out[...] = (
        refs.hidden[1]
        + wide(refs.inverse[1, own_tokens, :], D // LANES) * summed(refs.landed.at[1], tc)
    ).astype(BF16)
    grads_done()
    d_mixed = dot(grads_all[:, :D], refs.weights[0, :, out_at:])
    inner_dot = jnp.broadcast_to(
        jnp.sum(grads_all[:, D:].astype(F32), axis=1, keepdims=True), (T, LANES)
    )
    finish, gradients0 = backward(0, grads_all[:, :D], d_mixed, inner_dot)
    finish()
    refs.d_x[...] = norm_back(0, refs.grad[...])
    small0 = start_small(0)
    small1()
    small0()
    for l in range(layers):
        refs.small_out[l, t] = summed(refs.small_all.at[l], dc)
    small_last = [start_blocks(refs.small_out.at[l], TP) for l in range(layers)]
    if gather_weights:
        maps_last = []
        for l, gradients in ((1, gradients1), (0, gradients0)):
            gradients()
            for part in range(2):
                refs.d_out[l, part] = summed(refs.got.at[l, part], half)
            refs.maps[l, t] = refs.d_out[l, 1, :, inner : inner + 2 * state_width].astype(BF16)
            maps_last.append(start_blocks(refs.maps.at[l], TP))
        for done in maps_last:
            done()
        for l in range(layers):
            refs.maps_out[l] = summed(refs.maps.at[l], tc)
    for done in small_last:
        done()
    return lx.used


def local(
    x_in,
    segment_ids,
    norm_gain,
    w_zx,
    w_dt,
    w_bc,
    conv_x,
    conv_x_bias,
    conv_bc,
    conv_bc_bias,
    dt_bias,
    a_log,
    d_skip,
    gate_gain,
    w_out,
    cotangent,
):
    layers, D = norm_gain.shape
    tc, dc = lax.axis_size(TP), lax.axis_size(DP)
    R = x_in.shape[0]
    T = segment_ids.shape[0]
    inner = conv_x.shape[2]
    heads = dt_bias.shape[1]
    state_pair = w_bc.shape[2]
    state_width = state_pair // 2
    head_width = inner // heads
    conv_width = inner + state_pair
    dt_at = inner + conv_width
    out_at = dt_at + LANES
    columns = out_at + inner
    depth = w_bc.shape[1]
    gather_weights = depth % 16 == 0
    bc_at = 2 * inner

    packed = jnp.concatenate(
        [
            w_zx.reshape(layers, depth, bc_at),
            w_bc,
            jnp.pad(w_dt, ((0, 0), (0, 0), (0, LANES - heads))),
            jnp.swapaxes(w_out, 1, 2),
        ],
        axis=2,
    )
    if not gather_weights:
        packed = lax.all_gather(packed, DP, axis=1, tiled=True)

    def line(value):
        value = value if value.ndim == 3 else value[:, None, :]
        return jnp.pad(value, ((0, 0), (0, 0), (0, D - value.shape[2])))

    params = jnp.concatenate(
        [
            line(jnp.concatenate([conv_x, conv_bc], axis=2)),
            line(jnp.concatenate([conv_x_bias, conv_bc_bias], axis=1)),
            line(gate_gain),
            line(norm_gain),
            line(dt_bias),
            line(a_log),
            line(jnp.repeat(d_skip, head_width, axis=1)),
            jnp.zeros((layers, 6, D), F32),
        ],
        axis=1,
    )
    segs = segment_ids.astype(F32)
    seg_col = jnp.broadcast_to(segs[:, None], (T, LANES))
    seg_row = jnp.broadcast_to(segs[None, :], (8, T))

    ext_rows = T + HALO
    S = jax.ShapeDtypeStruct
    ins = dict(
        x_in=x_in, cotangent=cotangent, packed=packed, params=params, seg_col=seg_col, seg_row=seg_row
    )
    outs = dict(
        y_out=S((R, D), BF16),
        d_x=S((R, D), F32),
        small_out=S((layers, tc, 8, D), F32),
    )
    if gather_weights:
        outs.update(
            d_out=S((layers, 2, depth, columns // 2), F32), maps_out=S((layers, depth, state_pair), F32)
        )
    else:
        outs.update(
            d_first=S((layers, D, columns // 2), BF16), d_second=S((layers, D, columns // 2), BF16)
        )
    scratch = dict(
        spread=((LANES, inner), BF16),
        below=((T, T), BF16),
        seg_ext=((ext_rows, LANES), F32),
        masks=((3, T, LANES), F32),
        bias=((T, T), F32),
        reached=((T, LANES), F32),
        kept=((T, LANES), F32),
        x_all=((ext_rows, D), BF16),
        cot_all=((T, D), BF16),
        normed=((layers, ext_rows, D), BF16),
        hidden=((layers, R, D), F32),
        ext=((layers, ext_rows, conv_width), F32),
        pre=((layers, T, conv_width), F32),
        act=((layers, T, conv_width), F32),
        z=((layers, T, inner), F32),
        dtb=((layers, T, LANES), F32),
        decay=((layers, T, LANES), F32),
        step_wide=((layers, T, inner), F32),
        from_start=((layers, T, inner), F32),
        to_end=((layers, T, inner), F32),
        end_decay=((layers, 1, inner), F32),
        scaled=((layers, T, inner), BF16),
        bmat=((layers, T, state_width), BF16),
        cmat=((layers, T, state_width), BF16),
        states=((layers, dc, state_width + HALO, inner), BF16),
        coefs=((layers, dc, 8, inner), F32),
        scores=((layers, T, T), F32),
        spans=((layers, heads, T, T), F32),
        mixing=((layers, heads, T, T), BF16),
        ssd=((layers, T, inner), F32),
        start=((layers, state_width, inner), F32),
        partial=((layers, T, D), BF16),
        landed=((layers, tc, R, D), BF16),
        tokens=((layers, tc, 16, T), F32),
        inverse=((layers, T, LANES), F32),
        unscaled=((R, D), F32),
        d_all=((ext_rows, out_at), BF16),
        d_low=((ext_rows, state_pair), BF16),
        d_ssd=((T, inner), BF16),
        d_scaled=((T, inner), F32),
        d_rows=((layers, ext_rows, D), BF16),
        d_landed=((layers, tc, R, D), BF16),
        d_heads=((layers, tc, HALO, D), BF16),
        d_own=((R, D), F32),
        grad=((R, D), F32),
        grads_all=((T, D + LANES), BF16),
        small=((layers, 8, D), F32),
        small_all=((layers, dc, 8, D), F32),
    )
    if gather_weights:
        scratch.update(
            weights=((layers, D, columns), BF16),
            d_first=((layers, D, columns // 2), BF16),
            d_second=((layers, D, columns // 2), BF16),
            pairs=((layers, 2, dc // 2, depth, columns // 2), BF16),
            got=((layers, 2, dc // 2, depth, columns // 2), BF16),
            maps=((layers, tc, depth, state_pair), BF16),
        )
    names = list(ins) + list(outs) + list(scratch) + ["send", "recv"]
    sizes = (layers, T, D, inner, conv_width, dc, tc, gather_weights, state_width)
    semaphores = 16 * dc + 24 * tc if gather_weights else 8 * dc + 24 * tc

    def kernel(*args):
        refs = types.SimpleNamespace(**dict(zip(names, args)))
        if not gather_weights:
            refs.weights = refs.packed
        refs.head_width = head_width
        used = whole_step(sizes, refs)
        assert used <= semaphores, used

    vmem = pl.BlockSpec(memory_space=pltpu.VMEM)
    results = pl.pallas_call(
        kernel,
        out_shape=tuple(outs.values()),
        in_specs=[vmem] * len(ins),
        out_specs=tuple([vmem] * len(outs)),
        scratch_shapes=[pltpu.VMEM(shape, kind) for shape, kind in scratch.values()]
        + [pltpu.SemaphoreType.DMA((semaphores,))] * 2,
        compiler_params=pltpu.CompilerParams(
            collective_id=1, has_side_effects=True, vmem_limit_bytes=60 * 1024 * 1024
        ),
    )(*ins.values())
    found = dict(zip(outs, results))
    if gather_weights:
        d_out, d_maps = found["d_out"], found["maps_out"]
    else:
        d_out = jnp.stack(
            [
                lax.psum_scatter(found[n].astype(F32), DP, scatter_dimension=1, tiled=True)
                for n in ("d_first", "d_second")
            ],
            axis=1,
        )
        d_maps = lax.psum(d_out[:, 1, :, inner : inner + state_pair], TP)
    small = found["small_out"]

    def joined_up(at, begin, width, count=1):
        piece = jnp.moveaxis(small[:, :, at : at + count, begin : begin + width], 1, 2)
        piece = piece.reshape(layers, count, tc * width)
        return piece if count > 1 else piece[:, 0]

    total = jnp.sum(small, axis=1)
    return (
        found["y_out"],
        found["d_x"],
        total[:, 6],
        jnp.swapaxes(d_out[:, :, :, :inner], 1, 2),
        d_out[:, 1, :, inner + state_pair : inner + state_pair + heads],
        d_maps,
        joined_up(0, 0, inner, conv_x.shape[1]),
        joined_up(4, 0, inner),
        total[:, 0:4, inner:conv_width],
        total[:, 4, inner:conv_width],
        joined_up(0, conv_width, heads),
        joined_up(1, conv_width, heads),
        joined_up(2, conv_width, heads),
        joined_up(5, 0, inner),
        jnp.swapaxes(d_out[:, 0, :, inner:], 1, 2),
    )


def solution(mesh):
    return jax.shard_map(
        local,
        mesh=mesh,
        in_specs=(
            P((DP, TP), None),
            P(DP),
            P(),
            P(None, DP, None, TP),
            P(None, DP, TP),
            P(None, DP, None),
            P(None, None, TP),
            P(None, TP),
            P(),
            P(),
            P(None, TP),
            P(None, TP),
            P(None, TP),
            P(None, TP),
            P(None, TP, DP),
            P((DP, TP), None),
        ),
        out_specs=(
            P((DP, TP), None),
            P((DP, TP), None),
            P(),
            P(None, DP, None, TP),
            P(None, DP, TP),
            P(None, DP, None),
            P(),
            P(),
            P(),
            P(),
            P(),
            P(),
            P(),
            P(),
            P(None, TP, DP),
        ),
        check_vma=False,
    )
```

```python
import types

import jax
import jax.numpy as jnp
from jax import lax
from jax.experimental import pallas as pl
from jax.experimental.pallas import tpu as pltpu
from jax.sharding import PartitionSpec as P

EPSILON = 1e-05
MESH = pl.DeviceIdType.MESH
DP, TP = "dp", "tensor"
F32 = jnp.float32
BF16 = jnp.bfloat16
HALO = 16
LANES = 128


def pieces(value, count):
    found = []
    for _ in range(count):
        high = value.astype(BF16)
        found.append(high)
        value = value - high.astype(F32)
    return found


def dot(a, b, over_a=1, over_b=0):
    return lax.dot_general(
        a, b, (((over_a,), (over_b,)), ((), ())), preferred_element_type=F32
    )


def fine_dot(a, exact, over_a=1, over_b=0, count=3):
    return sum(dot(part, exact, over_a, over_b) for part in pieces(a, count))


def wide(value, times):
    return jnp.concatenate([value] * times, axis=1)


def sigmoid(v):
    return 1.0 / (1.0 + jnp.exp(-v))


class Links:
    def __init__(self, send, recv):
        self.send, self.recv, self.used = send, recv, 0

    def take(self, count=1):
        self.used += count
        return self.used - count

    def copy(self, src, dst, device, send_at, recv_at):
        return pltpu.make_async_remote_copy(
            src_ref=src,
            dst_ref=dst,
            send_sem=self.send.at[send_at],
            recv_sem=self.recv.at[recv_at],
            device_id=device,
            device_id_type=MESH,
        )


def whole_step(sizes, refs):
    layers, T, D, inner, conv_width, dc, tc, gather_weights, state_width = sizes
    R = T // tc
    ext_rows = T + HALO
    bc_at = 2 * inner
    dt_at = inner + conv_width
    out_at = dt_at + LANES
    columns = out_at + inner
    full_inner = inner * tc
    head_width = refs.head_width
    per = LANES // head_width
    chunks = inner // LANES
    depth = D // dc
    lx = Links(refs.send, refs.recv)
    a, t = lax.axis_index(DP), lax.axis_index(TP)
    last_t = tc - 1
    prev, following = lax.rem(a + dc - 1, dc), lax.rem(a + 1, dc)
    half = dc // 2
    core = lax.rem(a, 2)
    sibling = a + 1 - 2 * core

    barrier = pltpu.get_barrier_semaphore()
    greeted = 0
    for s in range(1, tc):
        pl.semaphore_signal(
            barrier, inc=1, device_id={DP: a, TP: lax.rem(t + s, tc)}, device_id_type=MESH
        )
        greeted += 1
    for s in range(1, dc):
        near = s == 1 or s == dc - 1
        for u in range(tc if near else 1):
            pl.semaphore_signal(
                barrier,
                inc=1,
                device_id={DP: lax.rem(a + s, dc), TP: lax.rem(t + u, tc)},
                device_id_type=MESH,
            )
            greeted += 1

    lane = lax.broadcasted_iota(jnp.int32, (1, LANES), 1)
    low_half = lane < head_width
    spread = refs.spread
    rows_i = lax.broadcasted_iota(jnp.int32, (LANES, inner), 0)
    cols_i = lax.broadcasted_iota(jnp.int32, (LANES, inner), 1)
    spread[...] = (
        (cols_i >= rows_i * head_width) & (cols_i < (rows_i + 1) * head_width)
    ).astype(F32).astype(BF16)
    below = refs.below
    tri_i = lax.broadcasted_iota(jnp.int32, (T, T), 0)
    tri_j = lax.broadcasted_iota(jnp.int32, (T, T), 1)
    below[...] = (tri_i >= tri_j).astype(F32).astype(BF16)
    seg_ext, masks, bias = refs.seg_ext, refs.masks, refs.bias
    seg_row = refs.segs[...].astype(F32)
    seg_col = jnp.broadcast_to(seg_row, (LANES, T)).T
    seg_ext[HALO:, :] = seg_col
    inside = (wide(seg_col, T // LANES) == seg_row) & (tri_i >= tri_j)
    bias[...] = jnp.where(inside, 0.0, -1e30)

    def own_rows(ref, offset=0):
        return ref.at[pl.ds(pl.multiple_of(offset + t * R, 16), R)]

    def start_rows(ref, offset, halo):
        base = lx.take(tc + (2 * tc if halo else 0))
        sent = []
        if halo:
            for u in range(tc):
                c = lx.copy(
                    ref.at[pl.ds(T, HALO)],
                    ref.at[pl.ds(0, HALO)],
                    {DP: following, TP: jnp.int32(u)},
                    base + tc + u,
                    base + tc,
                )
                pl.when(t == last_t)(c.start)
        for s in range(1, tc):
            c = lx.copy(
                own_rows(ref, offset),
                own_rows(ref, offset),
                {DP: a, TP: lax.rem(t + s, tc)},
                base + s,
                base + s,
            )
            c.start()
            sent.append(c)

        def finish():
            for c in sent:
                c.wait()
            if halo:
                for u in range(tc):
                    c = lx.copy(
                        ref.at[pl.ds(T, HALO)],
                        ref.at[pl.ds(0, HALO)],
                        {DP: following, TP: jnp.int32(u)},
                        base + tc + u,
                        base + tc,
                    )
                    pl.when(t == last_t)(c.wait_send)
                c.wait_recv()

        return finish

    def start_blocks(ref, axis):
        count, me = (dc, a) if axis == DP else (tc, t)
        base = lx.take(count)
        sent = []
        for s in range(1, count):
            c = lx.copy(
                ref.at[me],
                ref.at[me],
                {DP: a, TP: t, axis: lax.rem(me + s, count)},
                base + s,
                base + s,
            )
            c.start()
            sent.append(c)

        def finish():
            for c in sent:
                c.wait()

        return finish

    def start_shared(view):
        base = lx.take(dc)
        own = lx.copy(view(a), view(a), {DP: sibling, TP: t}, base, base)
        across = []
        for s in range(1, half):
            peer = lax.rem(a + 2 * s, dc)
            c = lx.copy(view(a), view(a), {DP: peer, TP: t}, base + s, base + s)
            c.start()
            across.append(c)
        own.start()

        def finish():
            passed = []
            for s in range(1, half):
                across[s - 1].wait_recv()
                source = lax.rem(a + dc - 2 * s, dc)
                c = lx.copy(
                    view(source), view(source), {DP: sibling, TP: t}, base + half + s, base + half + s
                )
                c.start()
                passed.append(c)
            own.wait()
            for c in across:
                c.wait_send()
            for c in passed:
                c.wait()

        return finish

    def start_pairs(source, pairs, got):
        base = lx.take(dc)
        sent = []
        for k in range(half):
            c = lx.copy(
                source.at[depth_block(2 * k + 1 - core)],
                pairs.at[k],
                {DP: sibling, TP: t},
                base + k,
                base + k,
            )
            c.start()
            sent.append(c)

        def second():
            for c in sent:
                c.wait()
            across = []
            for s in range(1, half + 1):
                peer = lax.rem(a + 2 * s, dc)
                k = peer // 2
                total = source[depth_block(peer), :].astype(F32) + pairs[k].astype(F32)
                if s == half:
                    got[a // 2] = total.astype(BF16)
                    continue
                pairs[k] = total.astype(BF16)
                c = lx.copy(
                    pairs.at[k],
                    got.at[a // 2],
                    {DP: peer, TP: t},
                    base + half + s,
                    base + half + s,
                )
                c.start()
                across.append(c)

            def finish():
                for c in across:
                    c.wait()

            return finish

        return second

    def start_owners(source, block_of, ref, axis):
        count, me = (dc, a) if axis == DP else (tc, t)
        base = lx.take(count)
        sent = []
        for s in range(1, count):
            peer = lax.rem(me + s, count)
            c = lx.copy(
                source.at[block_of(peer)],
                ref.at[me],
                {DP: a, TP: t, axis: peer},
                base + s,
                base + s,
            )
            c.start()
            sent.append(c)
        ref[me] = source[block_of(me)]

        def finish():
            for c in sent:
                c.wait()

        return finish

    def token_block(offset):
        return lambda peer: pl.ds(pl.multiple_of(offset + peer * R, 16), R)

    def depth_block(peer):
        return pl.ds(pl.multiple_of(peer * depth, 16), depth)

    def start_weights(l):
        ref = refs.weights.at[l]
        cols = pl.ds(0, out_at), pl.ds(out_at, inner)
        return [start_shared(lambda i, c=c: ref.at[depth_block(i), c]) for c in cols]

    params = refs.params
    heads = refs.dt_bias.shape[1]
    eye_i = lax.broadcasted_iota(jnp.int32, (depth, depth), 0)
    eye_j = lax.broadcasted_iota(jnp.int32, (depth, depth), 1)
    eye = (eye_i == eye_j).astype(F32).astype(BF16)
    for l in range(layers):
        params[l] = jnp.zeros_like(params[l])
        params[l, 0:4, :inner] = refs.conv_x[l]
        params[l, 0:4, inner:conv_width] = refs.conv_bc[l]
        params[l, 4:5, :inner] = refs.conv_x_bias[l : l + 1, :]
        params[l, 4:5, inner:conv_width] = refs.conv_bc_bias[l : l + 1, :]
        params[l, 5:6, :inner] = refs.gate_gain[l : l + 1, :]
        params[l, 6:7, :] = refs.norm_gain[l : l + 1, :]
        params[l, 7:8, :heads] = refs.dt_bias[l : l + 1, :]
        params[l, 8:9, :heads] = refs.a_log[l : l + 1, :]
        params[l, 10:11, :heads] = refs.d_skip[l : l + 1, :]
        params[l, 8:16, :inner] = jnp.where(
            lax.broadcasted_iota(jnp.int32, (8, inner), 0) == 1,
            pltpu.roll(fine_dot(params[l, 8:16, :LANES], spread[...]), 7, 0),
            params[l, 8:16, :inner],
        )
        if gather_weights:
            W = refs.weights.at[l]
            mine = depth_block(a)
            W[mine, :inner] = refs.w_zx[l, :, 0, :]
            W[mine, inner:bc_at] = refs.w_zx[l, :, 1, :]
            W[mine, bc_at:dt_at] = refs.w_bc[l]
            W[mine, dt_at:out_at] = jnp.zeros((depth, LANES), BF16)
            W[mine, dt_at : dt_at + heads] = dot(eye, refs.w_dt[:, l, :], 1, 1).astype(BF16)
            W[mine, out_at:] = refs.w_out[l]

    own_x = own_rows(refs.x_all, HALO)
    own_x[...] = refs.x_in[...]
    own_c = own_rows(refs.cot_all)
    own_c[...] = refs.cotangent[...]

    pl.semaphore_wait(barrier, greeted)

    seg_base = lx.take()
    seg_copy = lx.copy(
        seg_ext.at[pl.ds(T, HALO)],
        seg_ext.at[pl.ds(0, HALO)],
        {DP: following, TP: t},
        seg_base,
        seg_base,
    )
    seg_copy.start()
    rows_done = start_rows(refs.x_all, HALO, True)
    nothing = [lambda: None] * 2
    weights_done = start_weights(0) if gather_weights else nothing
    seg_copy.wait()
    seg_ext[0:HALO, :] = jnp.where(a == 0, -1.0, seg_ext[0:HALO, :])
    for k in range(3):
        masks[k] = (seg_ext[pl.ds(HALO - 3 + k, T), :] == seg_col).astype(F32)
    first_seg, last_seg = seg_ext[HALO : HALO + 1, :], seg_ext[ext_rows - 1 :, :]
    reached = (seg_col == first_seg).astype(F32)
    kept = (seg_col == last_seg).astype(F32)
    joined = wide((seg_ext[HALO - 1 : HALO, :] == first_seg).astype(F32), chunks)
    whole_seg = wide((last_seg == first_seg).astype(F32), chunks)
    refs.reached[...] = reached
    refs.kept[...] = kept
    rows_done()

    def row(l, at, width):
        return refs.params[l, at : at + 1, :width]

    def norm_rows(h, gain):
        scale = lax.rsqrt(jnp.mean(h * h, axis=1, keepdims=True) + EPSILON)
        return (h * scale * gain).astype(BF16)

    refs.normed[0] = norm_rows(refs.x_all[...].astype(F32), row(0, 6, D))
    refs.hidden[0] = own_x[...].astype(F32)

    def as_column(value):
        return fine_dot(value, jnp.full((8, LANES), 0.125, BF16), 0, 0)

    def row_sums(value):
        return fine_dot_rows(value)

    def fine_dot_rows(value):
        ones = jnp.ones((8, inner), BF16)
        return sum(dot(ones, part, 1, 1) for part in pieces(value, 2))

    def forward(l):
        W = refs.weights.at[l]
        nx, ext, pre, act = (r.at[l] for r in (refs.normed, refs.ext, refs.pre, refs.act))
        tokens = pl.ds(HALO, T)
        refs.z[l] = dot(nx[tokens, :], W[:, :inner])
        ext[...] = dot(nx[...], W[:, inner:dt_at]).astype(BF16).astype(F32)
        dtb = dot(nx[tokens, :], W[:, dt_at:out_at]) + row(l, 7, LANES)
        for c in range(conv_width // LANES):
            at = slice(c * LANES, (c + 1) * LANES)
            taps = refs.params[l, 0:5, at]
            total = taps[4:5] + taps[3:4] * ext[tokens, at]
            for k in range(3):
                total = total + taps[k : k + 1] * ext[pl.ds(HALO - 3 + k, T), at] * masks[k]
            pre[:, at] = total
            act[:, at] = total * sigmoid(total)
        step = jnp.maximum(dtb, 0.0) + jnp.log1p(jnp.exp(-jnp.abs(dtb)))
        decay = -step * jnp.exp(row(l, 8, LANES))
        cum = sum(dot(below[...], part) for part in pieces(decay, 3))
        refs.dtb[l] = dtb
        refs.decay[l] = decay
        step_wide = fine_dot(step, spread[...])
        cum_wide = fine_dot(cum, spread[...])
        end = cum_wide[T - 1 :, :]
        from_start = jnp.exp(cum_wide) * wide(refs.reached[...], chunks)
        to_end = jnp.exp(end - cum_wide) * wide(refs.kept[...], chunks)
        refs.step_wide[l] = step_wide
        refs.from_start[l] = from_start
        refs.to_end[l] = to_end
        end_decay = jnp.exp(end)
        refs.end_decay[l] = end_decay
        xs = act[:, :inner]
        scaled = xs * step_wide
        refs.scaled[l] = scaled.astype(BF16)
        bmat = act[:, inner : inner + state_width].astype(BF16)
        cmat = act[:, inner + state_width :].astype(BF16)
        refs.bmat[l] = bmat
        refs.cmat[l] = cmat
        states, coefs = refs.states.at[l], refs.coefs.at[l]
        states[a, :state_width] = dot(bmat, (scaled * to_end).astype(BF16), 0, 0).astype(BF16)
        parts = pieces(joined * whole_seg * end_decay, 3)
        states[a, state_width:] = jnp.concatenate(
            parts + [jnp.zeros((13, inner), BF16)], axis=0
        )
        states_done = start_shared(lambda i: states.at[i])
        scores = dot(cmat, bmat, 1, 1)
        refs.scores[l] = scores
        cum_rows = cum.T
        for c in range(chunks):
            at = slice(c * LANES, (c + 1) * LANES)
            pair = refs.scaled[l, :, at]
            found = []
            for u in range(per):
                h = c * per + u
                span = cum[:, h : h + 1] - cum_rows[h : h + 1, :] + bias[...]
                kernel_h = jnp.exp(span)
                refs.spans[l, h] = kernel_h
                mixed_h = (kernel_h * scores).astype(BF16)
                refs.mixing[l, h] = mixed_h
                found.append(dot(mixed_h, pair))
            refs.ssd[l, :, at] = choose(found) + row(l, 9, inner)[:, at] * act[:, at]
        states_done()

        def keep(s, carry):
            coefs[s] = jnp.broadcast_to(
                jnp.sum(states[s, state_width:].astype(F32), axis=0, keepdims=True), (8, inner)
            )
            return carry

        lax.fori_loop(0, dc, keep, 0)
        return states, coefs

    def choose(found):
        result = found[0]
        for u in range(1, per):
            result = jnp.where(lane < u * head_width, result, found[u])
        return result

    def enter(values, coefs, backward):
        def step(i, state):
            s = dc - 1 - i if backward else i
            ahead = s > a if backward else s < a
            later = values[s, :state_width].astype(F32) + coefs[s][0:1, :] * state
            return jnp.where(ahead, later, state)

        return lax.fori_loop(0, dc, step, jnp.zeros((state_width, inner), F32))

    def gate(l, states, coefs):
        start = joined * enter(states, coefs, False)
        refs.start[l] = start
        refs.ssd[l] = refs.ssd[l] + refs.from_start[l] * dot(
            refs.cmat[l], start.astype(BF16)
        )
        z = refs.z[l]
        return refs.ssd[l] * (z * sigmoid(z))

    def project_out(l, gated):
        W = refs.weights.at[l]
        unscaled = (gated * row(l, 5, inner)).astype(BF16)
        refs.partial[l] = dot(unscaled, W[:, out_at:], 1, 1).astype(BF16)
        return start_owners(refs.partial.at[l], token_block(0), refs.landed.at[l], TP)

    def summed(ref, count):
        total = ref[0].astype(F32)
        for s in range(1, count):
            total = total + ref[s].astype(F32)
        return total

    def inverse_from(l):
        squares = summed(refs.tokens.at[l], tc)
        inverse = lax.rsqrt(squares[0:8] / full_inner + EPSILON)
        refs.inverse[l] = as_column(inverse)
        return squares

    own_tokens = pl.ds(pl.multiple_of(t * R, 16), R)

    weights_done[0]()
    states, coefs = forward(0)
    weights_done[1]()
    weights_done = start_weights(1) if gather_weights else nothing
    cot_done = start_rows(refs.cot_all, 0, False)
    gated = gate(0, states, coefs)
    refs.tokens[0, t] = jnp.concatenate([fine_dot_rows(gated * gated)] * 2, axis=0)
    squares_done = start_blocks(refs.tokens.at[0], TP)
    branch_done = project_out(0, gated)
    squares_done()
    inverse_from(0)
    branch_done()
    branch = summed(refs.landed.at[0], tc)
    refs.unscaled[...] = branch
    h1 = refs.hidden[0] + wide(refs.inverse[0, own_tokens, :], D // LANES) * branch
    refs.hidden[1] = h1
    own_n = own_rows(refs.normed.at[1], HALO)
    own_n[...] = norm_rows(h1, row(1, 6, D))
    rows_done = start_rows(refs.normed.at[1], HALO, True)
    cot_done()
    for done in weights_done:
        done()
    rows_done()
    states, coefs = forward(1)
    W1 = refs.weights.at[1]
    d_mixed = dot(refs.cot_all[...], W1[:, out_at:])
    gated = gate(1, states, coefs)
    refs.tokens[1, t] = jnp.concatenate(
        [fine_dot_rows(gated * gated), fine_dot_rows(d_mixed * gated * row(1, 5, inner))], axis=0
    )
    squares_done = start_blocks(refs.tokens.at[1], TP)
    out_done = project_out(1, gated)
    squares_done()
    totals = inverse_from(1)
    inner_dot = as_column(totals[8:16])

    def head_sums(value, count=2):
        return sum(dot(part, spread[...], 1, 1) for part in pieces(value, count))

    def put_small(l, at, value, lane_at=0):
        refs.small[l, at : at + value.shape[0], lane_at : lane_at + value.shape[1]] = value

    def column_sum(value):
        return jnp.sum(value, axis=0, keepdims=True)

    def backward(l, grad_rows, d_mixed, inner_dot):
        W = refs.weights.at[l]
        nx, ext, pre, act = (r.at[l] for r in (refs.normed, refs.ext, refs.pre, refs.act))
        d_all, d_low = refs.d_all, refs.d_low
        z, ssd = refs.z[l], refs.ssd[l]
        sig = sigmoid(z)
        silu = z * sig
        gated = ssd * silu
        inverse = wide(refs.inverse[l], chunks)
        gain = row(l, 5, inner)
        scaled_gate = gated * inverse
        mixed = (scaled_gate * gain).astype(BF16)
        put_small(l, 5, column_sum(d_mixed * scaled_gate))
        d_gated = inverse * gain * d_mixed - scaled_gate * inverse * inverse * (
            wide(inner_dot, chunks) / full_inner
        )
        tokens = pl.ds(HALO, T)
        d_all[0:HALO, 0:inner] = jnp.zeros((HALO, inner), BF16)
        d_all[0:HALO, dt_at:out_at] = jnp.zeros((HALO, LANES), BF16)
        d_all[tokens, 0:inner] = (d_gated * ssd * sig * (1.0 + z * (1.0 - sig))).astype(BF16)
        d_ssd = d_gated * silu
        d_ssd_low = d_ssd.astype(BF16)
        refs.d_ssd[...] = d_ssd_low
        from_start = (d_ssd * refs.from_start[l]).astype(BF16)
        d_states = refs.states.at[layers - 1 - l]
        cmat, bmat = refs.cmat[l], refs.bmat[l]
        d_states[a, :state_width] = (joined * dot(cmat, from_start, 0, 0)).astype(BF16)
        d_states_done = start_shared(lambda i: d_states.at[i, pl.ds(0, state_width)])
        start = refs.start[l]
        d_scores = jnp.zeros((T, T), F32)
        for c in range(chunks):
            at = slice(c * LANES, (c + 1) * LANES)
            pair, d_pair = refs.scaled[l, :, at], refs.d_ssd[:, at]
            found = []
            for u in range(per):
                h = c * per + u
                here = (lane >= u * head_width) & (lane < (u + 1) * head_width)
                d_mixing = dot(jnp.where(here, d_pair, jnp.zeros_like(d_pair)), pair, 1, 1)
                d_scores = d_scores + d_mixing * refs.spans[l, h]
                found.append(dot(refs.mixing[l, h], d_pair, 0, 0))
            refs.d_scaled[:, at] = choose(found)
        d_scores = d_scores.astype(BF16)
        d_cmat = dot(d_scores, bmat) + dot(from_start, start.astype(BF16), 1, 1)
        d_bmat = dot(d_scores, cmat, 0, 0)
        d_first, d_second = refs.d_first.at[l], refs.d_second.at[l]
        d_first[:, :inner] = dot(nx[...], d_all[:, :inner], 0, 0).astype(BF16)
        d_first[:, inner:] = dot(grad_rows, mixed, 0, 0).astype(BF16)
        d_states_done()
        if gather_weights:
            second = start_pairs(d_first, refs.pairs.at[l, 0], refs.got.at[l, 0])
        d_end = enter(d_states, refs.coefs.at[l], True)
        d_end_low = d_end.astype(BF16)
        to_end = refs.to_end[l]
        scaled_low = refs.scaled[l].astype(F32)
        from_end = to_end * dot(bmat, d_end_low)
        d_scaled = refs.d_scaled[...] + from_end
        d_bmat = d_bmat + dot((scaled_low * to_end).astype(BF16), d_end_low, 1, 1)
        xs = act[:, :inner]
        skip = row(l, 9, inner)
        d_cum = d_ssd_low.astype(F32) * (ssd - skip * xs) - scaled_low * d_scaled
        d_last = column_sum(scaled_low * from_end) + whole_seg * refs.end_decay[
            l
        ] * column_sum(d_end * start)
        is_last = lax.broadcasted_iota(jnp.int32, (T, inner), 0) == T - 1
        d_cum = head_sums(d_cum + jnp.where(is_last, d_last, 0.0), 3)
        d_decay = sum(dot(below[...], part, 0, 0) for part in pieces(d_cum, 3))
        d_step = head_sums(xs * d_scaled) - d_decay * jnp.exp(row(l, 8, LANES))
        d_dt = d_step * sigmoid(refs.dtb[l])
        d_all[tokens, dt_at:out_at] = d_dt.astype(BF16)
        put_small(l, 0, column_sum(d_dt), conv_width)
        put_small(l, 1, column_sum(d_decay * refs.decay[l]), conv_width)
        put_small(l, 2, head_sums(jnp.broadcast_to(column_sum(xs * d_ssd), (8, inner)))[0:1], conv_width)
        d_xs = refs.step_wide[l] * d_scaled + skip * d_ssd
        for c in range(conv_width // LANES):
            at = slice(c * LANES, (c + 1) * LANES)
            if c < chunks:
                d_act = d_xs[:, at]
            else:
                both = jnp.concatenate([d_bmat, d_cmat], axis=1)
                d_act = both[:, (c - chunks) * LANES : (c - chunks + 1) * LANES]
            p = pre[:, at]
            s = sigmoid(p)
            d_pre = d_act * s * (1.0 + p * (1.0 - s))
            taps = refs.params[l, 0:5, at]
            top = jnp.zeros((HALO, LANES), F32)
            put_small(l, 4, column_sum(d_pre), c * LANES)
            put_small(l, 3, column_sum(d_pre * ext[tokens, at]), c * LANES)
            d_ext = jnp.concatenate([top, d_pre * taps[3:4]], axis=0)
            for k in range(3):
                part = d_pre * masks[k]
                put_small(
                    l, k, column_sum(part * ext[pl.ds(HALO - 3 + k, T), at]), c * LANES
                )
                moved = jnp.concatenate([top, part * taps[k : k + 1]], axis=0)
                d_ext = d_ext + pltpu.roll(moved, ext_rows - 3 + k, 0)
            at_all = slice(inner + c * LANES, inner + (c + 1) * LANES)
            high = d_ext.astype(BF16)
            d_all[:, at_all] = high
            if c >= chunks:
                d_low[:, (c - chunks) * LANES : (c - chunks + 1) * LANES] = (
                    d_ext - high.astype(F32)
                ).astype(BF16)
        rows = dot(d_all[...], W[:, :out_at], 1, 1) + dot(d_low[...], W[:, bc_at:dt_at], 1, 1)
        refs.d_rows[l] = rows.astype(BF16)
        done = start_owners(
            refs.d_rows.at[l], token_block(HALO), refs.d_landed.at[l], TP
        )
        base = lx.take(tc + 1)

        def head_copy():
            return lx.copy(
                refs.d_rows.at[l].at[pl.ds(0, HALO)],
                refs.d_heads.at[l].at[t],
                {DP: prev, TP: jnp.int32(last_t)},
                base + tc,
                base + t,
            )

        head_copy().start()

        if gather_weights:
            first_done = second()
        maps = pl.ds(0, 2 * state_width)
        d_second[:, maps] = (
            dot(nx[...], d_all[:, bc_at:dt_at], 0, 0) + dot(nx[...], d_low[...], 0, 0)
        ).astype(BF16)
        d_second[:, 2 * state_width : inner] = dot(nx[...], d_all[:, dt_at:out_at], 0, 0).astype(
            BF16
        )
        halves = [pl.ds(0, inner), pl.ds(inner, inner)]

        def start_second(cols):
            return start_pairs(
                d_second.at[:, cols], refs.pairs.at[l, 1, :, :, cols], refs.got.at[l, 1, :, :, cols]
            )

        if gather_weights:
            second = start_second(halves[0])
        d_second[:, inner:] = dot(nx[...], d_all[:, inner:bc_at], 0, 0).astype(BF16)
        if gather_weights:
            maps_done = second()
            second = start_second(halves[1])
            second_done = second()

        def gradients():
            maps_done()
            refs.maps[l, t] = summed(refs.got.at[l, 1, :, :, maps], half).astype(BF16)
            maps_sent = start_blocks(refs.maps.at[l], TP)
            first_done()
            put_out(l, 0, summed(refs.got.at[l, 0], half))
            second_done()
            put_out(l, 1, summed(refs.got.at[l, 1], half))

            def last():
                maps_sent()
                put_maps(l, summed(refs.maps.at[l], tc))

            return last

        def finish():
            done()
            head_copy().wait_send()

            @pl.when(t == last_t)
            def _():
                for u in range(tc):
                    lx.copy(
                        refs.d_rows.at[l].at[pl.ds(0, HALO)],
                        refs.d_heads.at[l].at[u],
                        {DP: prev, TP: jnp.int32(last_t)},
                        base + tc,
                        base + u,
                    ).wait_recv()

            refs.d_own[...] = summed(refs.d_landed.at[l], tc)

            @pl.when(t == last_t)
            def _():
                refs.d_own[R - HALO :, :] = refs.d_own[R - HALO :, :] + summed(
                    refs.d_heads.at[l], tc
                )

        return finish, gradients

    results = refs.results
    small_at, grads_at = 2 * R, 2 * R + layers * tc * 8
    maps_at = grads_at + layers * 2 * depth

    def put_out(l, part, value):
        at = grads_at + (2 * l + part) * depth
        results[at : at + depth, :] = value

    def put_maps(l, value):
        at = maps_at + l * depth
        results[at : at + depth, 0 : 2 * state_width] = value
        results[at : at + depth, 2 * state_width :] = jnp.zeros((depth, D - 2 * state_width), F32)

    def norm_back(l, grad):
        h, d = refs.hidden[l], refs.d_own[...]
        scale = lax.rsqrt(jnp.mean(h * h, axis=1, keepdims=True) + EPSILON)
        put_small(l, 6, column_sum(d * h * scale))
        weighted = d * row(l, 6, D)
        return (
            grad
            + scale * weighted
            - h * scale * scale * scale * jnp.mean(weighted * h, axis=1, keepdims=True)
        )

    for l in range(layers):
        refs.small[l] = jnp.zeros_like(refs.small[l])

    def start_small(l):
        refs.small_all[l, a] = refs.small[l]
        return start_blocks(refs.small_all.at[l], DP)

    finish, gradients1 = backward(1, refs.cot_all[...], d_mixed, inner_dot)
    finish()
    grad = norm_back(1, own_c[...].astype(F32))
    refs.grad[...] = grad
    grads_all = refs.grads_all
    low = grad.astype(BF16)
    here = own_rows(grads_all)
    here[:, :D] = low
    dots = jnp.sum(low.astype(F32) * refs.unscaled[...], axis=1, keepdims=True)
    high, mid, rest = pieces(jnp.broadcast_to(dots, (R, LANES)), 3)
    zero = jnp.zeros_like(high)
    here[:, D:] = jnp.where(
        lane == 0, high, jnp.where(lane == 1, mid, jnp.where(lane == 2, rest, zero))
    )
    grads_done = start_rows(grads_all, 0, False)
    small1 = start_small(1)
    out_done()
    results[0:R, :] = (
        refs.hidden[1]
        + wide(refs.inverse[1, own_tokens, :], D // LANES) * summed(refs.landed.at[1], tc)
    )
    grads_done()
    d_mixed = dot(grads_all[:, :D], refs.weights[0, :, out_at:])
    inner_dot = jnp.broadcast_to(
        jnp.sum(grads_all[:, D:].astype(F32), axis=1, keepdims=True), (T, LANES)
    )
    finish, gradients0 = backward(0, grads_all[:, :D], d_mixed, inner_dot)
    if gather_weights:
        last1 = gradients1()
    finish()
    results[R : 2 * R, :] = norm_back(0, refs.grad[...])
    small0 = start_small(0)
    small1()
    refs.small_out[1, t] = summed(refs.small_all.at[1], dc)
    sent1 = start_blocks(refs.small_out.at[1], TP)
    small0()
    refs.small_out[0, t] = summed(refs.small_all.at[0], dc)
    sent0 = start_blocks(refs.small_out.at[0], TP)
    if gather_weights:
        last0 = gradients0()
        last1()
        last0()
    sent1()
    sent0()
    for l in range(layers):
        for u in range(tc):
            at = small_at + (l * tc + u) * 8
            results[at : at + 8, :] = refs.small_out[l, u]
    return lx.used


def local(
    x_in,
    segment_ids,
    norm_gain,
    w_zx,
    w_dt,
    w_bc,
    conv_x,
    conv_x_bias,
    conv_bc,
    conv_bc_bias,
    dt_bias,
    a_log,
    d_skip,
    gate_gain,
    w_out,
    cotangent,
):
    layers, D = norm_gain.shape
    tc, dc = lax.axis_size(TP), lax.axis_size(DP)
    R = x_in.shape[0]
    T = segment_ids.shape[0]
    inner = conv_x.shape[2]
    heads = dt_bias.shape[1]
    state_pair = w_bc.shape[2]
    state_width = state_pair // 2
    head_width = inner // heads
    conv_width = inner + state_pair
    dt_at = inner + conv_width
    out_at = dt_at + LANES
    columns = out_at + inner
    depth = w_bc.shape[1]
    gather_weights = depth % 16 == 0
    bc_at = 2 * inner

    ins = dict(
        x_in=x_in,
        cotangent=cotangent,
        segs=segment_ids.reshape(1, T),
        norm_gain=norm_gain,
        conv_x=conv_x,
        conv_x_bias=conv_x_bias,
        conv_bc=conv_bc,
        conv_bc_bias=conv_bc_bias,
        dt_bias=dt_bias,
        a_log=a_log,
        d_skip=d_skip,
        gate_gain=gate_gain,
    )
    if gather_weights:
        ins.update(
            w_zx=w_zx,
            w_bc=w_bc,
            w_dt=jnp.transpose(w_dt, (2, 0, 1)),
            w_out=jnp.swapaxes(w_out, 1, 2),
        )
    else:
        packed = jnp.concatenate(
            [
                w_zx.reshape(layers, depth, bc_at),
                w_bc,
                jnp.pad(w_dt, ((0, 0), (0, 0), (0, LANES - heads))),
                jnp.swapaxes(w_out, 1, 2),
            ],
            axis=2,
        )
        ins.update(weights=lax.all_gather(packed, DP, axis=1, tiled=True))

    ext_rows = T + HALO
    S = jax.ShapeDtypeStruct
    grads_rows = layers * 3 * depth if gather_weights else 0
    outs = dict(results=S((2 * R + layers * tc * 8 + grads_rows, D), F32))
    if not gather_weights:
        outs.update(d_first=S((layers, D, D), BF16), d_second=S((layers, D, D), BF16))
    scratch = dict(
        spread=((LANES, inner), BF16),
        params=((layers, 16, D), F32),
        below=((T, T), BF16),
        seg_ext=((ext_rows, LANES), F32),
        masks=((3, T, LANES), F32),
        bias=((T, T), F32),
        reached=((T, LANES), F32),
        kept=((T, LANES), F32),
        x_all=((ext_rows, D), BF16),
        cot_all=((T, D), BF16),
        normed=((layers, ext_rows, D), BF16),
        hidden=((layers, R, D), F32),
        ext=((layers, ext_rows, conv_width), F32),
        pre=((layers, T, conv_width), F32),
        act=((layers, T, conv_width), F32),
        z=((layers, T, inner), F32),
        dtb=((layers, T, LANES), F32),
        decay=((layers, T, LANES), F32),
        step_wide=((layers, T, inner), F32),
        from_start=((layers, T, inner), F32),
        to_end=((layers, T, inner), F32),
        end_decay=((layers, 1, inner), F32),
        scaled=((layers, T, inner), BF16),
        bmat=((layers, T, state_width), BF16),
        cmat=((layers, T, state_width), BF16),
        states=((layers, dc, state_width + HALO, inner), BF16),
        coefs=((layers, dc, 8, inner), F32),
        scores=((layers, T, T), F32),
        spans=((layers, heads, T, T), F32),
        mixing=((layers, heads, T, T), BF16),
        ssd=((layers, T, inner), F32),
        start=((layers, state_width, inner), F32),
        partial=((layers, T, D), BF16),
        landed=((layers, tc, R, D), BF16),
        tokens=((layers, tc, 16, T), F32),
        inverse=((layers, T, LANES), F32),
        unscaled=((R, D), F32),
        d_all=((ext_rows, out_at), BF16),
        d_low=((ext_rows, state_pair), BF16),
        d_ssd=((T, inner), BF16),
        d_scaled=((T, inner), F32),
        d_rows=((layers, ext_rows, D), BF16),
        d_landed=((layers, tc, R, D), BF16),
        d_heads=((layers, tc, HALO, D), BF16),
        d_own=((R, D), F32),
        grad=((R, D), F32),
        grads_all=((T, D + LANES), BF16),
        small=((layers, 8, D), F32),
        small_out=((layers, tc, 8, D), F32),
        small_all=((layers, dc, 8, D), F32),
    )
    if gather_weights:
        scratch.update(
            weights=((layers, D, columns), BF16),
            d_first=((layers, D, columns // 2), BF16),
            d_second=((layers, D, columns // 2), BF16),
            pairs=((layers, 2, dc // 2, depth, columns // 2), BF16),
            got=((layers, 2, dc // 2, depth, columns // 2), BF16),
            maps=((layers, tc, depth, state_pair), BF16),
        )
    names = list(ins) + list(outs) + list(scratch) + ["send", "recv"]
    sizes = (layers, T, D, inner, conv_width, dc, tc, gather_weights, state_width)
    semaphores = 16 * dc + 24 * tc if gather_weights else 8 * dc + 24 * tc

    def kernel(*args):
        refs = types.SimpleNamespace(**dict(zip(names, args)))
        refs.head_width = head_width
        used = whole_step(sizes, refs)
        assert used <= semaphores, used

    vmem = pl.BlockSpec(memory_space=pltpu.VMEM)
    results = pl.pallas_call(
        kernel,
        out_shape=tuple(outs.values()),
        in_specs=[vmem] * len(ins),
        out_specs=tuple([vmem] * len(outs)),
        scratch_shapes=[pltpu.VMEM(shape, kind) for shape, kind in scratch.values()]
        + [pltpu.SemaphoreType.DMA((semaphores,))] * 2,
        compiler_params=pltpu.CompilerParams(
            collective_id=1, has_side_effects=True, vmem_limit_bytes=60 * 1024 * 1024
        ),
    )(*ins.values())
    found = dict(zip(outs, results))
    small_at, grads_at = 2 * R, 2 * R + layers * tc * 8
    room_of = depth + -depth % 8
    maps_at = grads_at + layers * 2 * room_of
    all_results = found["results"]
    if not gather_weights:
        d_out = jnp.stack(
            [
                lax.psum_scatter(found[n].astype(F32), DP, scatter_dimension=1, tiled=True)
                for n in ("d_first", "d_second")
            ],
            axis=1,
        )
        d_maps = lax.psum(d_out[:, 1, :, :state_pair], TP)
        fill = (0, room_of - depth)
        d_out = jnp.pad(d_out, ((0, 0), (0, 0), fill, (0, 0))).reshape(-1, D)
        d_maps = jnp.pad(d_maps, ((0, 0), fill, (0, D - state_pair))).reshape(-1, D)
        all_results = jnp.concatenate([all_results, d_out, d_maps], axis=0)
    lasts = (
        S((R, D), BF16),
        S((R, D), F32),
        S((layers, D), F32),
        S((layers, depth, 2, inner), F32),
        S((heads, layers, depth), F32),
        S((layers, depth, state_pair), F32),
        S((layers, conv_x.shape[1], tc * inner), F32),
        S((layers, tc * inner), F32),
        S(conv_bc.shape, F32),
        S(conv_bc_bias.shape, F32),
        S((layers, tc * heads), F32),
        S((layers, tc * heads), F32),
        S((layers, tc * heads), F32),
        S((layers, tc * inner), F32),
        S((layers, depth, inner), F32),
    )

    def unpack(found, *refs):
        y, dx, dgain, dzx, ddt, dbc, dcx, dcxb, dcb, dcbb, ddtb, dal, dsk, dgate, dwo, room = refs
        y[...] = found[0:R, :].astype(BF16)
        dx[...] = found[R : 2 * R, :]
        taps = conv_x.shape[1]
        for l in range(layers):
            at = slice(l, l + 1)
            small = [found.at[pl.ds(small_at + (l * tc + u) * 8, 8)] for u in range(tc)]
            first = pl.ds(grads_at + 2 * l * room_of, depth)
            second = pl.ds(grads_at + (2 * l + 1) * room_of, depth)
            dgain[at, :] = sum(small[u][6:7, :] for u in range(tc))
            dcb[l] = sum(small[u][0:taps, inner:conv_width] for u in range(tc))
            dcbb[at, :] = sum(small[u][4:5, inner:conv_width] for u in range(tc))
            rows = jnp.zeros((8, LANES), F32)
            for u in range(tc):
                cols = slice(u * inner, (u + 1) * inner)
                dcx[l, :, cols] = small[u][0:taps, :inner]
                dcxb[at, cols] = small[u][4:5, :inner]
                dgate[at, cols] = small[u][5:6, :inner]
                rows = rows + pltpu.roll(small[u][:, conv_width:], u * heads, 1)
            ddtb[at, :] = rows[0:1, : tc * heads]
            dal[at, :] = rows[1:2, : tc * heads]
            dsk[at, :] = rows[2:3, : tc * heads]
            dbc[l] = found[pl.ds(maps_at + l * room_of, depth), :state_pair]
            room[0:depth, :] = found[second, state_pair:inner]
            ddt[:, l, :] = room[...].T[:heads, :depth]
            dzx[l, :, 0, :] = found[first, :inner]
            dzx[l, :, 1, :] = found[second, inner:]
            dwo[l] = found[first, inner:]

    last = pl.pallas_call(
        unpack,
        out_shape=lasts,
        in_specs=[vmem],
        out_specs=tuple([vmem] * len(lasts)),
        scratch_shapes=[pltpu.VMEM((LANES, LANES), F32)],
        compiler_params=pltpu.CompilerParams(vmem_limit_bytes=32 * 1024 * 1024),
    )(all_results)
    return last[:4] + (jnp.transpose(last[4], (1, 2, 0)),) + last[5:14] + (jnp.swapaxes(last[14], 1, 2),)


def solution(mesh):
    return jax.shard_map(
        local,
        mesh=mesh,
        in_specs=(
            P((DP, TP), None),
            P(DP),
            P(),
            P(None, DP, None, TP),
            P(None, DP, TP),
            P(None, DP, None),
            P(None, None, TP),
            P(None, TP),
            P(),
            P(),
            P(None, TP),
            P(None, TP),
            P(None, TP),
            P(None, TP),
            P(None, TP, DP),
            P((DP, TP), None),
        ),
        out_specs=(
            P((DP, TP), None),
            P((DP, TP), None),
            P(),
            P(None, DP, None, TP),
            P(None, DP, TP),
            P(None, DP, None),
            P(),
            P(),
            P(),
            P(),
            P(),
            P(),
            P(),
            P(),
            P(None, TP, DP),
        ),
        check_vma=False,
    )
```

```python
import types

import jax
import jax.numpy as jnp
from jax import lax
from jax.experimental import pallas as pl
from jax.experimental.pallas import tpu as pltpu
from jax.sharding import PartitionSpec as P

EPSILON = 1e-05
MESH = pl.DeviceIdType.MESH
DP, TP = "dp", "tensor"
F32 = jnp.float32
BF16 = jnp.bfloat16
HALO = 16
LANES = 128


def pieces(value, count):
    found = []
    for _ in range(count):
        high = value.astype(BF16)
        found.append(high)
        value = value - high.astype(F32)
    return found


def dot(a, b, over_a=1, over_b=0):
    return lax.dot_general(
        a, b, (((over_a,), (over_b,)), ((), ())), preferred_element_type=F32
    )


def fine_dot(a, exact, over_a=1, over_b=0, count=3):
    return sum(dot(part, exact, over_a, over_b) for part in pieces(a, count))


def wide(value, times):
    return jnp.concatenate([value] * times, axis=1)


def sigmoid(v):
    return 1.0 / (1.0 + jnp.exp(-v))


class Links:
    def __init__(self, send, recv):
        self.send, self.recv, self.used = send, recv, 0

    def take(self, count=1):
        self.used += count
        return self.used - count

    def copy(self, src, dst, device, send_at, recv_at):
        return pltpu.make_async_remote_copy(
            src_ref=src,
            dst_ref=dst,
            send_sem=self.send.at[send_at],
            recv_sem=self.recv.at[recv_at],
            device_id=device,
            device_id_type=MESH,
        )


def whole_step(sizes, refs):
    layers, T, D, inner, conv_width, dc, tc, gather_weights, state_width = sizes
    R = T // tc
    ext_rows = T + HALO
    bc_at = 2 * inner
    dt_at = inner + conv_width
    out_at = dt_at + LANES
    columns = out_at + inner
    full_inner = inner * tc
    head_width = refs.head_width
    per = LANES // head_width
    chunks = inner // LANES
    depth = D // dc
    lx = Links(refs.send, refs.recv)
    a, t = lax.axis_index(DP), lax.axis_index(TP)
    last_t = tc - 1
    prev, following = lax.rem(a + dc - 1, dc), lax.rem(a + 1, dc)
    half = dc // 2
    core = lax.rem(a, 2)
    sibling = a + 1 - 2 * core

    barrier = pltpu.get_barrier_semaphore()
    greeted = 0
    for s in range(1, tc):
        pl.semaphore_signal(
            barrier, inc=1, device_id={DP: a, TP: lax.rem(t + s, tc)}, device_id_type=MESH
        )
        greeted += 1
    for s in range(1, dc):
        near = s == 1 or s == dc - 1
        for u in range(tc if near else 1):
            pl.semaphore_signal(
                barrier,
                inc=1,
                device_id={DP: lax.rem(a + s, dc), TP: lax.rem(t + u, tc)},
                device_id_type=MESH,
            )
            greeted += 1

    lane = lax.broadcasted_iota(jnp.int32, (1, LANES), 1)
    low_half = lane < head_width
    spread = refs.spread
    rows_i = lax.broadcasted_iota(jnp.int32, (LANES, inner), 0)
    cols_i = lax.broadcasted_iota(jnp.int32, (LANES, inner), 1)
    spread[...] = (
        (cols_i >= rows_i * head_width) & (cols_i < (rows_i + 1) * head_width)
    ).astype(F32).astype(BF16)
    below = refs.below
    tri_i = lax.broadcasted_iota(jnp.int32, (T, T), 0)
    tri_j = lax.broadcasted_iota(jnp.int32, (T, T), 1)
    below[...] = (tri_i >= tri_j).astype(F32).astype(BF16)
    seg_ext, masks, bias = refs.seg_ext, refs.masks, refs.bias
    seg_row = refs.segs[...].astype(F32)
    seg_col = jnp.broadcast_to(seg_row, (LANES, T)).T
    seg_ext[HALO:, :] = seg_col
    inside = (wide(seg_col, T // LANES) == seg_row) & (tri_i >= tri_j)
    bias[...] = jnp.where(inside, 0.0, -1e30)

    def own_rows(ref, offset=0):
        return ref.at[pl.ds(pl.multiple_of(offset + t * R, 16), R)]

    def part_rows(ref, offset, part, parts):
        n = R // parts
        return ref.at[pl.ds(pl.multiple_of(offset + part * n + t * R, 16), n)]

    def start_rows(ref, offset, halo, part=0, parts=1):
        base = lx.take(tc + (2 * tc if halo else 0))
        sent = []
        if halo:
            for u in range(tc):
                c = lx.copy(
                    ref.at[pl.ds(T, HALO)],
                    ref.at[pl.ds(0, HALO)],
                    {DP: following, TP: jnp.int32(u)},
                    base + tc + u,
                    base + tc,
                )
                pl.when(t == last_t)(c.start)
        for s in range(1, tc):
            c = lx.copy(
                part_rows(ref, offset, part, parts),
                part_rows(ref, offset, part, parts),
                {DP: a, TP: lax.rem(t + s, tc)},
                base + s,
                base + s,
            )
            c.start()
            sent.append(c)

        def finish():
            for c in sent:
                c.wait()
            if halo:
                for u in range(tc):
                    c = lx.copy(
                        ref.at[pl.ds(T, HALO)],
                        ref.at[pl.ds(0, HALO)],
                        {DP: following, TP: jnp.int32(u)},
                        base + tc + u,
                        base + tc,
                    )
                    pl.when(t == last_t)(c.wait_send)
                c.wait_recv()

        return finish

    def start_blocks(ref, axis):
        count, me = (dc, a) if axis == DP else (tc, t)
        base = lx.take(count)
        sent = []
        for s in range(1, count):
            c = lx.copy(
                ref.at[me],
                ref.at[me],
                {DP: a, TP: t, axis: lax.rem(me + s, count)},
                base + s,
                base + s,
            )
            c.start()
            sent.append(c)

        def finish():
            for c in sent:
                c.wait()

        return finish

    def start_shared(view):
        base = lx.take(dc)
        own = lx.copy(view(a), view(a), {DP: sibling, TP: t}, base, base)
        across = []
        for s in range(1, half):
            peer = lax.rem(a + 2 * s, dc)
            c = lx.copy(view(a), view(a), {DP: peer, TP: t}, base + s, base + s)
            c.start()
            across.append(c)
        own.start()

        def finish():
            passed = []
            for s in range(1, half):
                across[s - 1].wait_recv()
                source = lax.rem(a + dc - 2 * s, dc)
                c = lx.copy(
                    view(source), view(source), {DP: sibling, TP: t}, base + half + s, base + half + s
                )
                c.start()
                passed.append(c)
            own.wait()
            for c in across:
                c.wait_send()
            for c in passed:
                c.wait()

        return finish

    def start_pairs(source, pairs, got):
        base = lx.take(dc)
        sent = []
        for k in range(half):
            c = lx.copy(
                source.at[depth_block(2 * k + 1 - core)],
                pairs.at[k],
                {DP: sibling, TP: t},
                base + k,
                base + k,
            )
            c.start()
            sent.append(c)

        def second():
            for c in sent:
                c.wait()
            across = []
            for s in range(1, half + 1):
                peer = lax.rem(a + 2 * s, dc)
                k = peer // 2
                total = source[depth_block(peer), :].astype(F32) + pairs[k].astype(F32)
                if s == half:
                    got[a // 2] = total.astype(BF16)
                    continue
                pairs[k] = total.astype(BF16)
                c = lx.copy(
                    pairs.at[k],
                    got.at[a // 2],
                    {DP: peer, TP: t},
                    base + half + s,
                    base + half + s,
                )
                c.start()
                across.append(c)

            def finish():
                for c in across:
                    c.wait()

            return finish

        return second

    def start_sums(source, offset, ref, parts=2):
        n = R // parts

        def block(peer, part):
            return pl.ds(pl.multiple_of(offset + part * n + peer * R, 16), n)

        waits = []
        for part in range(parts):
            base = lx.take(tc)
            here = pl.ds(part * n, n)
            sent = []
            for s in range(1, tc):
                peer = lax.rem(t + s, tc)
                c = lx.copy(
                    source.at[block(peer, part)],
                    ref.at[t, here],
                    {DP: a, TP: peer},
                    base + s,
                    base + s,
                )
                c.start()
                sent.append(c)
            ref[t, here] = source[block(t, part)]
            waits.append(sent)

        def finish(part):
            for c in waits[part]:
                c.wait()

        return finish

    def depth_block(peer):
        return pl.ds(pl.multiple_of(peer * depth, 16), depth)

    def start_weights(l):
        ref = refs.weights.at[l]
        cols = pl.ds(0, out_at), pl.ds(out_at, inner)
        return [start_shared(lambda i, c=c: ref.at[depth_block(i), c]) for c in cols]

    params = refs.params
    heads = refs.dt_bias.shape[1]
    eye_i = lax.broadcasted_iota(jnp.int32, (depth, depth), 0)
    eye_j = lax.broadcasted_iota(jnp.int32, (depth, depth), 1)
    eye = (eye_i == eye_j).astype(F32).astype(BF16)
    for l in range(layers):
        params[l] = jnp.zeros_like(params[l])
        params[l, 0:4, :inner] = refs.conv_x[l]
        params[l, 0:4, inner:conv_width] = refs.conv_bc[l]
        params[l, 4:5, :inner] = refs.conv_x_bias[l : l + 1, :]
        params[l, 4:5, inner:conv_width] = refs.conv_bc_bias[l : l + 1, :]
        params[l, 5:6, :inner] = refs.gate_gain[l : l + 1, :]
        params[l, 6:7, :] = refs.norm_gain[l : l + 1, :]
        params[l, 7:8, :heads] = refs.dt_bias[l : l + 1, :]
        params[l, 8:9, :heads] = refs.a_log[l : l + 1, :]
        params[l, 10:11, :heads] = refs.d_skip[l : l + 1, :]
        params[l, 8:16, :inner] = jnp.where(
            lax.broadcasted_iota(jnp.int32, (8, inner), 0) == 1,
            pltpu.roll(fine_dot(params[l, 8:16, :LANES], spread[...]), 7, 0),
            params[l, 8:16, :inner],
        )
        if gather_weights:
            W = refs.weights.at[l]
            mine = depth_block(a)
            W[mine, :inner] = refs.w_zx[l, :, 0, :]
            W[mine, inner:bc_at] = refs.w_zx[l, :, 1, :]
            W[mine, bc_at:dt_at] = refs.w_bc[l]
            W[mine, dt_at:out_at] = jnp.zeros((depth, LANES), BF16)
            W[mine, dt_at : dt_at + heads] = dot(eye, refs.w_dt[:, l, :], 1, 1).astype(BF16)
            W[mine, out_at:] = refs.w_out[l]

    own_x = own_rows(refs.x_all, HALO)
    own_x[...] = refs.x_in[...]
    own_c = own_rows(refs.cot_all)
    own_c[...] = refs.cotangent[...]

    pl.semaphore_wait(barrier, greeted)

    seg_base = lx.take()
    seg_copy = lx.copy(
        seg_ext.at[pl.ds(T, HALO)],
        seg_ext.at[pl.ds(0, HALO)],
        {DP: following, TP: t},
        seg_base,
        seg_base,
    )
    seg_copy.start()
    rows_done = start_rows(refs.x_all, HALO, True)
    nothing = [lambda: None] * 2
    weights_done = start_weights(0) if gather_weights else nothing
    seg_copy.wait()
    seg_ext[0:HALO, :] = jnp.where(a == 0, -1.0, seg_ext[0:HALO, :])
    for k in range(3):
        masks[k] = (seg_ext[pl.ds(HALO - 3 + k, T), :] == seg_col).astype(F32)
    first_seg, last_seg = seg_ext[HALO : HALO + 1, :], seg_ext[ext_rows - 1 :, :]
    reached = (seg_col == first_seg).astype(F32)
    kept = (seg_col == last_seg).astype(F32)
    joined = wide((seg_ext[HALO - 1 : HALO, :] == first_seg).astype(F32), chunks)
    whole_seg = wide((last_seg == first_seg).astype(F32), chunks)
    refs.reached[...] = reached
    refs.kept[...] = kept
    rows_done()

    def row(l, at, width):
        return refs.params[l, at : at + 1, :width]

    def norm_rows(h, gain):
        scale = lax.rsqrt(jnp.mean(h * h, axis=1, keepdims=True) + EPSILON)
        return (h * scale * gain).astype(BF16)

    refs.normed[0] = norm_rows(refs.x_all[...].astype(F32), row(0, 6, D))
    refs.hidden[0] = own_x[...].astype(F32)

    def as_column(value):
        return fine_dot(value, jnp.full((8, LANES), 0.125, BF16), 0, 0)

    def row_sums(value):
        return fine_dot_rows(value)

    def fine_dot_rows(value):
        ones = jnp.ones((8, inner), BF16)
        return sum(dot(ones, part, 1, 1) for part in pieces(value, 2))

    def forward(l):
        W = refs.weights.at[l]
        nx, ext, pre, act = (r.at[l] for r in (refs.normed, refs.ext, refs.pre, refs.act))
        tokens = pl.ds(HALO, T)
        refs.z[l] = dot(nx[tokens, :], W[:, :inner])
        ext[...] = dot(nx[...], W[:, inner:dt_at]).astype(BF16).astype(F32)
        dtb = dot(nx[tokens, :], W[:, dt_at:out_at]) + row(l, 7, LANES)
        for c in range(conv_width // LANES):
            at = slice(c * LANES, (c + 1) * LANES)
            taps = refs.params[l, 0:5, at]
            total = taps[4:5] + taps[3:4] * ext[tokens, at]
            for k in range(3):
                total = total + taps[k : k + 1] * ext[pl.ds(HALO - 3 + k, T), at] * masks[k]
            pre[:, at] = total
            act[:, at] = total * sigmoid(total)
        step = jnp.maximum(dtb, 0.0) + jnp.log1p(jnp.exp(-jnp.abs(dtb)))
        decay = -step * jnp.exp(row(l, 8, LANES))
        cum = sum(dot(below[...], part) for part in pieces(decay, 3))
        refs.dtb[l] = dtb
        refs.decay[l] = decay
        step_wide = fine_dot(step, spread[...])
        cum_wide = fine_dot(cum, spread[...])
        end = cum_wide[T - 1 :, :]
        from_start = jnp.exp(cum_wide) * wide(refs.reached[...], chunks)
        to_end = jnp.exp(end - cum_wide) * wide(refs.kept[...], chunks)
        refs.step_wide[l] = step_wide
        refs.from_start[l] = from_start
        refs.to_end[l] = to_end
        end_decay = jnp.exp(end)
        refs.end_decay[l] = end_decay
        xs = act[:, :inner]
        scaled = xs * step_wide
        refs.scaled[l] = scaled.astype(BF16)
        bmat = act[:, inner : inner + state_width].astype(BF16)
        cmat = act[:, inner + state_width :].astype(BF16)
        refs.bmat[l] = bmat
        refs.cmat[l] = cmat
        states, coefs = refs.states.at[l], refs.coefs.at[l]
        states[a, :state_width] = dot(bmat, (scaled * to_end).astype(BF16), 0, 0).astype(BF16)
        parts = pieces(joined * whole_seg * end_decay, 3)
        states[a, state_width:] = jnp.concatenate(
            parts + [jnp.zeros((13, inner), BF16)], axis=0
        )
        states_done = start_shared(lambda i: states.at[i])
        scores = dot(cmat, bmat, 1, 1)
        refs.scores[l] = scores
        cum_rows = cum.T
        for c in range(chunks):
            at = slice(c * LANES, (c + 1) * LANES)
            pair = refs.scaled[l, :, at]
            found = []
            for u in range(per):
                h = c * per + u
                span = cum[:, h : h + 1] - cum_rows[h : h + 1, :] + bias[...]
                kernel_h = jnp.exp(span)
                refs.spans[l, h] = kernel_h
                mixed_h = (kernel_h * scores).astype(BF16)
                refs.mixing[l, h] = mixed_h
                found.append(dot(mixed_h, pair))
            refs.ssd[l, :, at] = choose(found) + row(l, 9, inner)[:, at] * act[:, at]
        states_done()

        def keep(s, carry):
            coefs[s] = jnp.broadcast_to(
                jnp.sum(states[s, state_width:].astype(F32), axis=0, keepdims=True), (8, inner)
            )
            return carry

        lax.fori_loop(0, dc, keep, 0)
        return states, coefs

    def choose(found):
        result = found[0]
        for u in range(1, per):
            result = jnp.where(lane < u * head_width, result, found[u])
        return result

    def enter(values, coefs, backward):
        def step(i, state):
            s = dc - 1 - i if backward else i
            ahead = s > a if backward else s < a
            later = values[s, :state_width].astype(F32) + coefs[s][0:1, :] * state
            return jnp.where(ahead, later, state)

        return lax.fori_loop(0, dc, step, jnp.zeros((state_width, inner), F32))

    def gate(l, states, coefs):
        start = joined * enter(states, coefs, False)
        refs.start[l] = start
        refs.ssd[l] = refs.ssd[l] + refs.from_start[l] * dot(
            refs.cmat[l], start.astype(BF16)
        )
        z = refs.z[l]
        return refs.ssd[l] * (z * sigmoid(z))

    def project_out(l, gated, parts):
        W = refs.weights.at[l]
        unscaled = (gated * row(l, 5, inner)).astype(BF16)
        refs.partial[l] = dot(unscaled, W[:, out_at:], 1, 1).astype(BF16)
        return start_sums(refs.partial.at[l], 0, refs.landed.at[l], parts)

    def summed_rows(ref, count, rows):
        total = ref[0, rows].astype(F32)
        for s in range(1, count):
            total = total + ref[s, rows].astype(F32)
        return total

    def summed(ref, count):
        total = ref[0].astype(F32)
        for s in range(1, count):
            total = total + ref[s].astype(F32)
        return total

    def inverse_from(l):
        squares = summed(refs.tokens.at[l], tc)
        inverse = lax.rsqrt(squares[0:8] / full_inner + EPSILON)
        refs.inverse[l] = as_column(inverse)
        return squares

    own_tokens = pl.ds(pl.multiple_of(t * R, 16), R)

    cot_done = start_rows(refs.cot_all, 0, False)
    weights_done[0]()
    states, coefs = forward(0)
    weights_done[1]()
    weights_done = start_weights(1) if gather_weights else nothing
    gated = gate(0, states, coefs)
    refs.tokens[0, t] = jnp.concatenate([fine_dot_rows(gated * gated)] * 2, axis=0)
    squares_done = start_blocks(refs.tokens.at[0], TP)
    branch_done = project_out(0, gated, 2)
    squares_done()
    inverse_from(0)
    n = R // 2
    rows_done = []
    for part in range(2):
        branch_done(part)
        rows = pl.ds(part * n, n)
        tokens = pl.ds(pl.multiple_of(t * R + part * n, 16), n)
        branch = summed_rows(refs.landed.at[0], tc, rows)
        refs.unscaled[rows, :] = branch
        h1 = refs.hidden[0, rows] + wide(refs.inverse[0, tokens, :], D // LANES) * branch
        refs.hidden[1, rows] = h1
        own_n = part_rows(refs.normed.at[1], HALO, part, 2)
        own_n[...] = norm_rows(h1, row(1, 6, D))
        rows_done.append(start_rows(refs.normed.at[1], HALO, part == 1, part, 2))
    cot_done()
    for done in weights_done:
        done()
    for done in rows_done:
        done()
    states, coefs = forward(1)
    W1 = refs.weights.at[1]
    d_mixed = dot(refs.cot_all[...], W1[:, out_at:])
    gated = gate(1, states, coefs)
    refs.tokens[1, t] = jnp.concatenate(
        [fine_dot_rows(gated * gated), fine_dot_rows(d_mixed * gated * row(1, 5, inner))], axis=0
    )
    squares_done = start_blocks(refs.tokens.at[1], TP)
    out_done = project_out(1, gated, 1)
    squares_done()
    totals = inverse_from(1)
    inner_dot = as_column(totals[8:16])

    def head_sums(value, count=2):
        return sum(dot(part, spread[...], 1, 1) for part in pieces(value, count))

    def put_small(l, at, value, lane_at=0):
        refs.small[l, at : at + value.shape[0], lane_at : lane_at + value.shape[1]] = value

    def column_sum(value):
        return jnp.sum(value, axis=0, keepdims=True)

    def backward(l, grad_rows, d_mixed, inner_dot):
        W = refs.weights.at[l]
        nx, ext, pre, act = (r.at[l] for r in (refs.normed, refs.ext, refs.pre, refs.act))
        d_all, d_low = refs.d_all, refs.d_low
        z, ssd = refs.z[l], refs.ssd[l]
        sig = sigmoid(z)
        silu = z * sig
        gated = ssd * silu
        inverse = wide(refs.inverse[l], chunks)
        gain = row(l, 5, inner)
        scaled_gate = gated * inverse
        mixed = (scaled_gate * gain).astype(BF16)
        put_small(l, 5, column_sum(d_mixed * scaled_gate))
        d_gated = inverse * gain * d_mixed - scaled_gate * inverse * inverse * (
            wide(inner_dot, chunks) / full_inner
        )
        tokens = pl.ds(HALO, T)
        d_all[0:HALO, 0:inner] = jnp.zeros((HALO, inner), BF16)
        d_all[0:HALO, dt_at:out_at] = jnp.zeros((HALO, LANES), BF16)
        d_all[tokens, 0:inner] = (d_gated * ssd * sig * (1.0 + z * (1.0 - sig))).astype(BF16)
        d_ssd = d_gated * silu
        d_ssd_low = d_ssd.astype(BF16)
        refs.d_ssd[...] = d_ssd_low
        from_start = (d_ssd * refs.from_start[l]).astype(BF16)
        d_states = refs.states.at[layers - 1 - l]
        cmat, bmat = refs.cmat[l], refs.bmat[l]
        d_states[a, :state_width] = (joined * dot(cmat, from_start, 0, 0)).astype(BF16)
        d_states_done = start_shared(lambda i: d_states.at[i, pl.ds(0, state_width)])
        start = refs.start[l]
        d_scores = jnp.zeros((T, T), F32)
        for c in range(chunks):
            at = slice(c * LANES, (c + 1) * LANES)
            pair, d_pair = refs.scaled[l, :, at], refs.d_ssd[:, at]
            found = []
            for u in range(per):
                h = c * per + u
                here = (lane >= u * head_width) & (lane < (u + 1) * head_width)
                d_mixing = dot(jnp.where(here, d_pair, jnp.zeros_like(d_pair)), pair, 1, 1)
                d_scores = d_scores + d_mixing * refs.spans[l, h]
                found.append(dot(refs.mixing[l, h], d_pair, 0, 0))
            refs.d_scaled[:, at] = choose(found)
        d_scores = d_scores.astype(BF16)
        d_cmat = dot(d_scores, bmat) + dot(from_start, start.astype(BF16), 1, 1)
        d_bmat = dot(d_scores, cmat, 0, 0)
        d_first, d_second = refs.d_first.at[l], refs.d_second.at[l]
        d_first[:, :inner] = dot(nx[...], d_all[:, :inner], 0, 0).astype(BF16)
        d_first[:, inner:] = dot(grad_rows, mixed, 0, 0).astype(BF16)
        d_states_done()
        if gather_weights:
            second = start_pairs(d_first, refs.pairs.at[l, 0], refs.got.at[l, 0])
        d_end = enter(d_states, refs.coefs.at[l], True)
        d_end_low = d_end.astype(BF16)
        to_end = refs.to_end[l]
        scaled_low = refs.scaled[l].astype(F32)
        from_end = to_end * dot(bmat, d_end_low)
        d_scaled = refs.d_scaled[...] + from_end
        d_bmat = d_bmat + dot((scaled_low * to_end).astype(BF16), d_end_low, 1, 1)
        xs = act[:, :inner]
        skip = row(l, 9, inner)
        d_cum = d_ssd_low.astype(F32) * (ssd - skip * xs) - scaled_low * d_scaled
        d_last = column_sum(scaled_low * from_end) + whole_seg * refs.end_decay[
            l
        ] * column_sum(d_end * start)
        is_last = lax.broadcasted_iota(jnp.int32, (T, inner), 0) == T - 1
        d_cum = head_sums(d_cum + jnp.where(is_last, d_last, 0.0), 3)
        d_decay = sum(dot(below[...], part, 0, 0) for part in pieces(d_cum, 3))
        d_step = head_sums(xs * d_scaled) - d_decay * jnp.exp(row(l, 8, LANES))
        d_dt = d_step * sigmoid(refs.dtb[l])
        d_all[tokens, dt_at:out_at] = d_dt.astype(BF16)
        put_small(l, 0, column_sum(d_dt), conv_width)
        put_small(l, 1, column_sum(d_decay * refs.decay[l]), conv_width)
        put_small(l, 2, head_sums(jnp.broadcast_to(column_sum(xs * d_ssd), (8, inner)))[0:1], conv_width)
        d_xs = refs.step_wide[l] * d_scaled + skip * d_ssd
        for c in range(conv_width // LANES):
            at = slice(c * LANES, (c + 1) * LANES)
            if c < chunks:
                d_act = d_xs[:, at]
            else:
                both = jnp.concatenate([d_bmat, d_cmat], axis=1)
                d_act = both[:, (c - chunks) * LANES : (c - chunks + 1) * LANES]
            p = pre[:, at]
            s = sigmoid(p)
            d_pre = d_act * s * (1.0 + p * (1.0 - s))
            taps = refs.params[l, 0:5, at]
            top = jnp.zeros((HALO, LANES), F32)
            put_small(l, 4, column_sum(d_pre), c * LANES)
            put_small(l, 3, column_sum(d_pre * ext[tokens, at]), c * LANES)
            d_ext = jnp.concatenate([top, d_pre * taps[3:4]], axis=0)
            for k in range(3):
                part = d_pre * masks[k]
                put_small(
                    l, k, column_sum(part * ext[pl.ds(HALO - 3 + k, T), at]), c * LANES
                )
                moved = jnp.concatenate([top, part * taps[k : k + 1]], axis=0)
                d_ext = d_ext + pltpu.roll(moved, ext_rows - 3 + k, 0)
            at_all = slice(inner + c * LANES, inner + (c + 1) * LANES)
            high = d_ext.astype(BF16)
            d_all[:, at_all] = high
            if c >= chunks:
                d_low[:, (c - chunks) * LANES : (c - chunks + 1) * LANES] = (
                    d_ext - high.astype(F32)
                ).astype(BF16)
        rows = dot(d_all[...], W[:, :out_at], 1, 1) + dot(d_low[...], W[:, bc_at:dt_at], 1, 1)
        refs.d_rows[l] = rows.astype(BF16)
        done = start_sums(refs.d_rows.at[l], HALO, refs.d_landed.at[l])
        base = lx.take(tc + 1)

        def head_copy():
            return lx.copy(
                refs.d_rows.at[l].at[pl.ds(0, HALO)],
                refs.d_heads.at[l].at[t],
                {DP: prev, TP: jnp.int32(last_t)},
                base + tc,
                base + t,
            )

        head_copy().start()

        if gather_weights:
            first_done = second()
        maps = pl.ds(0, 2 * state_width)
        d_second[:, maps] = (
            dot(nx[...], d_all[:, bc_at:dt_at], 0, 0) + dot(nx[...], d_low[...], 0, 0)
        ).astype(BF16)
        d_second[:, 2 * state_width : inner] = dot(nx[...], d_all[:, dt_at:out_at], 0, 0).astype(
            BF16
        )
        halves = [pl.ds(0, inner), pl.ds(inner, inner)]

        def start_second(cols):
            return start_pairs(
                d_second.at[:, cols], refs.pairs.at[l, 1, :, :, cols], refs.got.at[l, 1, :, :, cols]
            )

        if gather_weights:
            second = start_second(halves[0])
        d_second[:, inner:] = dot(nx[...], d_all[:, inner:bc_at], 0, 0).astype(BF16)
        if gather_weights:
            maps_done = second()
            second = start_second(halves[1])
            second_done = second()

        def gradients():
            maps_done()
            refs.maps[l, t] = summed(refs.got.at[l, 1, :, :, maps], half).astype(BF16)
            maps_sent = start_blocks(refs.maps.at[l], TP)
            first_done()
            put_out(l, 0, summed(refs.got.at[l, 0], half))
            second_done()
            put_out(l, 1, summed(refs.got.at[l, 1], half))

            def last():
                maps_sent()
                put_maps(l, summed(refs.maps.at[l], tc))

            return last

        def finish(part):
            done(part)
            n = R // 2
            rows = pl.ds(part * n, n)
            refs.d_own[rows, :] = summed_rows(refs.d_landed.at[l], tc, rows)
            if part == 0:
                return
            head_copy().wait_send()

            @pl.when(t == last_t)
            def _():
                for u in range(tc):
                    lx.copy(
                        refs.d_rows.at[l].at[pl.ds(0, HALO)],
                        refs.d_heads.at[l].at[u],
                        {DP: prev, TP: jnp.int32(last_t)},
                        base + tc,
                        base + u,
                    ).wait_recv()
                refs.d_own[R - HALO :, :] = refs.d_own[R - HALO :, :] + summed(
                    refs.d_heads.at[l], tc
                )

        return finish, gradients

    results = refs.results
    small_at, grads_at = 2 * R, 2 * R + layers * tc * 8
    maps_at = grads_at + layers * 2 * depth

    def put_out(l, part, value):
        at = grads_at + (2 * l + part) * depth
        results[at : at + depth, :] = value

    def put_maps(l, value):
        at = maps_at + l * depth
        results[at : at + depth, 0 : 2 * state_width] = value
        results[at : at + depth, 2 * state_width :] = jnp.zeros((depth, D - 2 * state_width), F32)

    def norm_back(l, grad, rows):
        h, d = refs.hidden[l, rows], refs.d_own[rows, :]
        scale = lax.rsqrt(jnp.mean(h * h, axis=1, keepdims=True) + EPSILON)
        refs.small[l, 6:7, :] = refs.small[l, 6:7, :] + column_sum(d * h * scale)
        weighted = d * row(l, 6, D)
        return (
            grad
            + scale * weighted
            - h * scale * scale * scale * jnp.mean(weighted * h, axis=1, keepdims=True)
        )

    for l in range(layers):
        refs.small[l] = jnp.zeros_like(refs.small[l])

    def start_small(l):
        refs.small_all[l, a] = refs.small[l]
        return start_blocks(refs.small_all.at[l], DP)

    finish, gradients1 = backward(1, refs.cot_all[...], d_mixed, inner_dot)
    grads_all = refs.grads_all
    grads_done = []
    for part in range(2):
        finish(part)
        rows = pl.ds(part * n, n)
        first = part_rows(refs.cot_all, 0, part, 2)
        grad = norm_back(1, first[...].astype(F32), rows)
        refs.grad[rows, :] = grad
        low = grad.astype(BF16)
        here = part_rows(grads_all, 0, part, 2)
        here[:, :D] = low
        dots = jnp.sum(low.astype(F32) * refs.unscaled[rows, :], axis=1, keepdims=True)
        high, mid, rest = pieces(jnp.broadcast_to(dots, (n, LANES)), 3)
        zero = jnp.zeros_like(high)
        here[:, D:] = jnp.where(
            lane == 0, high, jnp.where(lane == 1, mid, jnp.where(lane == 2, rest, zero))
        )
        grads_done.append(start_rows(grads_all, 0, False, part, 2))
    small1 = start_small(1)
    out_done(0)
    results[0:R, :] = (
        refs.hidden[1]
        + wide(refs.inverse[1, own_tokens, :], D // LANES) * summed(refs.landed.at[1], tc)
    )
    for done in grads_done:
        done()
    d_mixed = dot(grads_all[:, :D], refs.weights[0, :, out_at:])
    inner_dot = jnp.broadcast_to(
        jnp.sum(grads_all[:, D:].astype(F32), axis=1, keepdims=True), (T, LANES)
    )
    finish, gradients0 = backward(0, grads_all[:, :D], d_mixed, inner_dot)
    if gather_weights:
        last1 = gradients1()
    for part in range(2):
        finish(part)
        rows = pl.ds(part * n, n)
        results[R + part * n : R + part * n + n, :] = norm_back(0, refs.grad[rows, :], rows)
    small0 = start_small(0)
    small1()
    refs.small_out[1, t] = summed(refs.small_all.at[1], dc)
    sent1 = start_blocks(refs.small_out.at[1], TP)
    small0()
    refs.small_out[0, t] = summed(refs.small_all.at[0], dc)
    sent0 = start_blocks(refs.small_out.at[0], TP)
    if gather_weights:
        last0 = gradients0()
        last1()
        last0()
    sent1()
    sent0()
    for l in range(layers):
        for u in range(tc):
            at = small_at + (l * tc + u) * 8
            results[at : at + 8, :] = refs.small_out[l, u]
    return lx.used


def local(
    x_in,
    segment_ids,
    norm_gain,
    w_zx,
    w_dt,
    w_bc,
    conv_x,
    conv_x_bias,
    conv_bc,
    conv_bc_bias,
    dt_bias,
    a_log,
    d_skip,
    gate_gain,
    w_out,
    cotangent,
):
    layers, D = norm_gain.shape
    tc, dc = lax.axis_size(TP), lax.axis_size(DP)
    R = x_in.shape[0]
    T = segment_ids.shape[0]
    inner = conv_x.shape[2]
    heads = dt_bias.shape[1]
    state_pair = w_bc.shape[2]
    state_width = state_pair // 2
    head_width = inner // heads
    conv_width = inner + state_pair
    dt_at = inner + conv_width
    out_at = dt_at + LANES
    columns = out_at + inner
    depth = w_bc.shape[1]
    gather_weights = depth % 16 == 0
    bc_at = 2 * inner

    ins = dict(
        x_in=x_in,
        cotangent=cotangent,
        segs=segment_ids.reshape(1, T),
        norm_gain=norm_gain,
        conv_x=conv_x,
        conv_x_bias=conv_x_bias,
        conv_bc=conv_bc,
        conv_bc_bias=conv_bc_bias,
        dt_bias=dt_bias,
        a_log=a_log,
        d_skip=d_skip,
        gate_gain=gate_gain,
    )
    if gather_weights:
        ins.update(
            w_zx=w_zx,
            w_bc=w_bc,
            w_dt=jnp.transpose(w_dt, (2, 0, 1)),
            w_out=jnp.swapaxes(w_out, 1, 2),
        )
    else:
        packed = jnp.concatenate(
            [
                w_zx.reshape(layers, depth, bc_at),
                w_bc,
                jnp.pad(w_dt, ((0, 0), (0, 0), (0, LANES - heads))),
                jnp.swapaxes(w_out, 1, 2),
            ],
            axis=2,
        )
        ins.update(weights=lax.all_gather(packed, DP, axis=1, tiled=True))

    ext_rows = T + HALO
    S = jax.ShapeDtypeStruct
    grads_rows = layers * 3 * depth if gather_weights else 0
    outs = dict(results=S((2 * R + layers * tc * 8 + grads_rows, D), F32))
    if not gather_weights:
        outs.update(d_first=S((layers, D, D), BF16), d_second=S((layers, D, D), BF16))
    scratch = dict(
        spread=((LANES, inner), BF16),
        params=((layers, 16, D), F32),
        below=((T, T), BF16),
        seg_ext=((ext_rows, LANES), F32),
        masks=((3, T, LANES), F32),
        bias=((T, T), F32),
        reached=((T, LANES), F32),
        kept=((T, LANES), F32),
        x_all=((ext_rows, D), BF16),
        cot_all=((T, D), BF16),
        normed=((layers, ext_rows, D), BF16),
        hidden=((layers, R, D), F32),
        ext=((layers, ext_rows, conv_width), F32),
        pre=((layers, T, conv_width), F32),
        act=((layers, T, conv_width), F32),
        z=((layers, T, inner), F32),
        dtb=((layers, T, LANES), F32),
        decay=((layers, T, LANES), F32),
        step_wide=((layers, T, inner), F32),
        from_start=((layers, T, inner), F32),
        to_end=((layers, T, inner), F32),
        end_decay=((layers, 1, inner), F32),
        scaled=((layers, T, inner), BF16),
        bmat=((layers, T, state_width), BF16),
        cmat=((layers, T, state_width), BF16),
        states=((layers, dc, state_width + HALO, inner), BF16),
        coefs=((layers, dc, 8, inner), F32),
        scores=((layers, T, T), F32),
        spans=((layers, heads, T, T), F32),
        mixing=((layers, heads, T, T), BF16),
        ssd=((layers, T, inner), F32),
        start=((layers, state_width, inner), F32),
        partial=((layers, T, D), BF16),
        landed=((layers, tc, R, D), BF16),
        tokens=((layers, tc, 16, T), F32),
        inverse=((layers, T, LANES), F32),
        unscaled=((R, D), F32),
        d_all=((ext_rows, out_at), BF16),
        d_low=((ext_rows, state_pair), BF16),
        d_ssd=((T, inner), BF16),
        d_scaled=((T, inner), F32),
        d_rows=((layers, ext_rows, D), BF16),
        d_landed=((layers, tc, R, D), BF16),
        d_heads=((layers, tc, HALO, D), BF16),
        d_own=((R, D), F32),
        grad=((R, D), F32),
        grads_all=((T, D + LANES), BF16),
        small=((layers, 8, D), F32),
        small_out=((layers, tc, 8, D), F32),
        small_all=((layers, dc, 8, D), F32),
    )
    if gather_weights:
        scratch.update(
            weights=((layers, D, columns), BF16),
            d_first=((layers, D, columns // 2), BF16),
            d_second=((layers, D, columns // 2), BF16),
            pairs=((layers, 2, dc // 2, depth, columns // 2), BF16),
            got=((layers, 2, dc // 2, depth, columns // 2), BF16),
            maps=((layers, tc, depth, state_pair), BF16),
        )
    names = list(ins) + list(outs) + list(scratch) + ["send", "recv"]
    sizes = (layers, T, D, inner, conv_width, dc, tc, gather_weights, state_width)
    semaphores = 20 * dc + 40 * tc if gather_weights else 8 * dc + 40 * tc

    def kernel(*args):
        refs = types.SimpleNamespace(**dict(zip(names, args)))
        refs.head_width = head_width
        used = whole_step(sizes, refs)
        assert used <= semaphores, used

    vmem = pl.BlockSpec(memory_space=pltpu.VMEM)
    results = pl.pallas_call(
        kernel,
        out_shape=tuple(outs.values()),
        in_specs=[vmem] * len(ins),
        out_specs=tuple([vmem] * len(outs)),
        scratch_shapes=[pltpu.VMEM(shape, kind) for shape, kind in scratch.values()]
        + [pltpu.SemaphoreType.DMA((semaphores,))] * 2,
        compiler_params=pltpu.CompilerParams(
            collective_id=1, has_side_effects=True, vmem_limit_bytes=60 * 1024 * 1024
        ),
    )(*ins.values())
    found = dict(zip(outs, results))
    small_at, grads_at = 2 * R, 2 * R + layers * tc * 8
    room_of = depth + -depth % 8
    maps_at = grads_at + layers * 2 * room_of
    all_results = found["results"]
    if not gather_weights:
        d_out = jnp.stack(
            [
                lax.psum_scatter(found[n].astype(F32), DP, scatter_dimension=1, tiled=True)
                for n in ("d_first", "d_second")
            ],
            axis=1,
        )
        d_maps = lax.psum(d_out[:, 1, :, :state_pair], TP)
        fill = (0, room_of - depth)
        d_out = jnp.pad(d_out, ((0, 0), (0, 0), fill, (0, 0))).reshape(-1, D)
        d_maps = jnp.pad(d_maps, ((0, 0), fill, (0, D - state_pair))).reshape(-1, D)
        all_results = jnp.concatenate([all_results, d_out, d_maps], axis=0)
    lasts = (
        S((R, D), BF16),
        S((R, D), F32),
        S((layers, D), F32),
        S((layers, depth, 2, inner), F32),
        S((heads, layers, depth), F32),
        S((layers, depth, state_pair), F32),
        S((layers, conv_x.shape[1], tc * inner), F32),
        S((layers, tc * inner), F32),
        S(conv_bc.shape, F32),
        S(conv_bc_bias.shape, F32),
        S((layers, tc * heads), F32),
        S((layers, tc * heads), F32),
        S((layers, tc * heads), F32),
        S((layers, tc * inner), F32),
        S((layers, depth, inner), F32),
    )

    def unpack(found, *refs):
        y, dx, dgain, dzx, ddt, dbc, dcx, dcxb, dcb, dcbb, ddtb, dal, dsk, dgate, dwo, room = refs
        y[...] = found[0:R, :].astype(BF16)
        dx[...] = found[R : 2 * R, :]
        taps = conv_x.shape[1]
        for l in range(layers):
            at = slice(l, l + 1)
            small = [found.at[pl.ds(small_at + (l * tc + u) * 8, 8)] for u in range(tc)]
            first = pl.ds(grads_at + 2 * l * room_of, depth)
            second = pl.ds(grads_at + (2 * l + 1) * room_of, depth)
            dgain[at, :] = sum(small[u][6:7, :] for u in range(tc))
            dcb[l] = sum(small[u][0:taps, inner:conv_width] for u in range(tc))
            dcbb[at, :] = sum(small[u][4:5, inner:conv_width] for u in range(tc))
            rows = jnp.zeros((8, LANES), F32)
            for u in range(tc):
                cols = slice(u * inner, (u + 1) * inner)
                dcx[l, :, cols] = small[u][0:taps, :inner]
                dcxb[at, cols] = small[u][4:5, :inner]
                dgate[at, cols] = small[u][5:6, :inner]
                rows = rows + pltpu.roll(small[u][:, conv_width:], u * heads, 1)
            ddtb[at, :] = rows[0:1, : tc * heads]
            dal[at, :] = rows[1:2, : tc * heads]
            dsk[at, :] = rows[2:3, : tc * heads]
            dbc[l] = found[pl.ds(maps_at + l * room_of, depth), :state_pair]
            room[0:depth, :] = found[second, state_pair:inner]
            ddt[:, l, :] = room[...].T[:heads, :depth]
            dzx[l, :, 0, :] = found[first, :inner]
            dzx[l, :, 1, :] = found[second, inner:]
            dwo[l] = found[first, inner:]

    last = pl.pallas_call(
        unpack,
        out_shape=lasts,
        in_specs=[vmem],
        out_specs=tuple([vmem] * len(lasts)),
        scratch_shapes=[pltpu.VMEM((LANES, LANES), F32)],
        compiler_params=pltpu.CompilerParams(vmem_limit_bytes=32 * 1024 * 1024),
    )(all_results)
    return last[:4] + (jnp.transpose(last[4], (1, 2, 0)),) + last[5:14] + (jnp.swapaxes(last[14], 1, 2),)


def solution(mesh):
    return jax.shard_map(
        local,
        mesh=mesh,
        in_specs=(
            P((DP, TP), None),
            P(DP),
            P(),
            P(None, DP, None, TP),
            P(None, DP, TP),
            P(None, DP, None),
            P(None, None, TP),
            P(None, TP),
            P(),
            P(),
            P(None, TP),
            P(None, TP),
            P(None, TP),
            P(None, TP),
            P(None, TP, DP),
            P((DP, TP), None),
        ),
        out_specs=(
            P((DP, TP), None),
            P((DP, TP), None),
            P(),
            P(None, DP, None, TP),
            P(None, DP, TP),
            P(None, DP, None),
            P(),
            P(),
            P(),
            P(),
            P(),
            P(),
            P(),
            P(),
            P(None, TP, DP),
        ),
        check_vma=False,
    )
```

```python
import types

import jax
import jax.numpy as jnp
from jax import lax
from jax.experimental import pallas as pl
from jax.experimental.pallas import tpu as pltpu
from jax.sharding import PartitionSpec as P

EPSILON = 1e-05
MESH = pl.DeviceIdType.MESH
DP, TP = "dp", "tensor"
F32 = jnp.float32
BF16 = jnp.bfloat16
HALO = 16
LANES = 128


def pieces(value, count):
    found = []
    for _ in range(count):
        high = value.astype(BF16)
        found.append(high)
        value = value - high.astype(F32)
    return found


def dot(a, b, over_a=1, over_b=0):
    return lax.dot_general(
        a, b, (((over_a,), (over_b,)), ((), ())), preferred_element_type=F32
    )


def fine_dot(a, exact, over_a=1, over_b=0, count=3):
    return sum(dot(part, exact, over_a, over_b) for part in pieces(a, count))


def wide(value, times):
    return jnp.concatenate([value] * times, axis=1)


def sigmoid(v):
    return 1.0 / (1.0 + jnp.exp(-v))


class Links:
    def __init__(self, send, recv):
        self.send, self.recv, self.used = send, recv, 0

    def take(self, count=1):
        self.used += count
        return self.used - count

    def copy(self, src, dst, device, send_at, recv_at):
        return pltpu.make_async_remote_copy(
            src_ref=src,
            dst_ref=dst,
            send_sem=self.send.at[send_at],
            recv_sem=self.recv.at[recv_at],
            device_id=device,
            device_id_type=MESH,
        )


def whole_step(sizes, refs):
    layers, T, D, inner, conv_width, dc, tc, gather_weights, state_width = sizes
    R = T // tc
    steps = R // HALO
    n = R // steps
    ext_rows = T + HALO
    bc_at = 2 * inner
    dt_at = inner + conv_width
    out_at = dt_at + LANES
    columns = out_at + inner
    full_inner = inner * tc
    head_width = refs.head_width
    per = LANES // head_width
    chunks = inner // LANES
    depth = D // dc
    lx = Links(refs.send, refs.recv)
    a, t = lax.axis_index(DP), lax.axis_index(TP)
    last_t = tc - 1
    prev, following = lax.rem(a + dc - 1, dc), lax.rem(a + 1, dc)
    half = dc // 2
    core = lax.rem(a, 2)
    sibling = a + 1 - 2 * core

    barrier = pltpu.get_barrier_semaphore()
    greeted = 0
    for s in range(1, tc):
        pl.semaphore_signal(
            barrier, inc=1, device_id={DP: a, TP: lax.rem(t + s, tc)}, device_id_type=MESH
        )
        greeted += 1
    for s in range(1, dc):
        near = s == 1 or s == dc - 1
        for u in range(tc if near else 1):
            pl.semaphore_signal(
                barrier,
                inc=1,
                device_id={DP: lax.rem(a + s, dc), TP: lax.rem(t + u, tc)},
                device_id_type=MESH,
            )
            greeted += 1

    lane = lax.broadcasted_iota(jnp.int32, (1, LANES), 1)
    low_half = lane < head_width
    spread = refs.spread
    rows_i = lax.broadcasted_iota(jnp.int32, (LANES, inner), 0)
    cols_i = lax.broadcasted_iota(jnp.int32, (LANES, inner), 1)
    spread[...] = (
        (cols_i >= rows_i * head_width) & (cols_i < (rows_i + 1) * head_width)
    ).astype(F32).astype(BF16)
    below = refs.below
    tri_i = lax.broadcasted_iota(jnp.int32, (T, T), 0)
    tri_j = lax.broadcasted_iota(jnp.int32, (T, T), 1)
    below[...] = (tri_i >= tri_j).astype(F32).astype(BF16)
    seg_ext, masks, bias = refs.seg_ext, refs.masks, refs.bias
    seg_row = refs.segs[...].astype(F32)
    seg_col = jnp.broadcast_to(seg_row, (LANES, T)).T
    seg_ext[HALO:, :] = seg_col
    inside = (wide(seg_col, T // LANES) == seg_row) & (tri_i >= tri_j)
    bias[...] = jnp.where(inside, 0.0, -1e30)

    def own_rows(ref, offset=0):
        return ref.at[pl.ds(pl.multiple_of(offset + t * R, 16), R)]

    def part_rows(ref, offset, part, parts):
        n = R // parts
        return ref.at[pl.ds(pl.multiple_of(offset + part * n + t * R, 16), n)]

    def start_rows(ref, offset, halo, part=0, parts=1):
        base = lx.take(tc + (2 * tc if halo else 0))
        sent = []
        if halo:
            for u in range(tc):
                c = lx.copy(
                    ref.at[pl.ds(T, HALO)],
                    ref.at[pl.ds(0, HALO)],
                    {DP: following, TP: jnp.int32(u)},
                    base + tc + u,
                    base + tc,
                )
                pl.when(t == last_t)(c.start)
        for s in range(1, tc):
            c = lx.copy(
                part_rows(ref, offset, part, parts),
                part_rows(ref, offset, part, parts),
                {DP: a, TP: lax.rem(t + s, tc)},
                base + s,
                base + s,
            )
            c.start()
            sent.append(c)

        def finish():
            for c in sent:
                c.wait()
            if halo:
                for u in range(tc):
                    c = lx.copy(
                        ref.at[pl.ds(T, HALO)],
                        ref.at[pl.ds(0, HALO)],
                        {DP: following, TP: jnp.int32(u)},
                        base + tc + u,
                        base + tc,
                    )
                    pl.when(t == last_t)(c.wait_send)
                c.wait_recv()

        return finish

    def start_blocks(ref, axis):
        count, me = (dc, a) if axis == DP else (tc, t)
        base = lx.take(count)
        sent = []
        for s in range(1, count):
            c = lx.copy(
                ref.at[me],
                ref.at[me],
                {DP: a, TP: t, axis: lax.rem(me + s, count)},
                base + s,
                base + s,
            )
            c.start()
            sent.append(c)

        def finish():
            for c in sent:
                c.wait()

        return finish

    def start_shared(view):
        base = lx.take(dc)
        own = lx.copy(view(a), view(a), {DP: sibling, TP: t}, base, base)
        across = []
        for s in range(1, half):
            peer = lax.rem(a + 2 * s, dc)
            c = lx.copy(view(a), view(a), {DP: peer, TP: t}, base + s, base + s)
            c.start()
            across.append(c)
        own.start()

        def finish():
            passed = []
            for s in range(1, half):
                across[s - 1].wait_recv()
                source = lax.rem(a + dc - 2 * s, dc)
                c = lx.copy(
                    view(source), view(source), {DP: sibling, TP: t}, base + half + s, base + half + s
                )
                c.start()
                passed.append(c)
            own.wait()
            for c in across:
                c.wait_send()
            for c in passed:
                c.wait()

        return finish

    def start_pairs(source, pairs, got):
        base = lx.take(dc)
        sent = []
        for k in range(half):
            c = lx.copy(
                source.at[depth_block(2 * k + 1 - core)],
                pairs.at[k],
                {DP: sibling, TP: t},
                base + k,
                base + k,
            )
            c.start()
            sent.append(c)

        def second():
            for c in sent:
                c.wait()
            across = []
            for s in range(1, half + 1):
                peer = lax.rem(a + 2 * s, dc)
                k = peer // 2
                total = source[depth_block(peer), :].astype(F32) + pairs[k].astype(F32)
                if s == half:
                    got[a // 2] = total.astype(BF16)
                    continue
                pairs[k] = total.astype(BF16)
                c = lx.copy(
                    pairs.at[k],
                    got.at[a // 2],
                    {DP: peer, TP: t},
                    base + half + s,
                    base + half + s,
                )
                c.start()
                across.append(c)

            def finish():
                for c in across:
                    c.wait()

            return finish

        return second

    def start_sums(source, offset, ref, parts):
        n = R // parts

        def block(peer, part):
            return pl.ds(pl.multiple_of(offset + part * n + peer * R, 16), n)

        waits = []
        for part in range(parts):
            base = lx.take(tc)
            here = pl.ds(part * n, n)
            sent = []
            for s in range(1, tc):
                peer = lax.rem(t + s, tc)
                c = lx.copy(
                    source.at[block(peer, part)],
                    ref.at[t, here],
                    {DP: a, TP: peer},
                    base + s,
                    base + s,
                )
                c.start()
                sent.append(c)
            ref[t, here] = source[block(t, part)]
            waits.append(sent)

        def finish(part):
            for c in waits[part]:
                c.wait()

        return finish

    def depth_block(peer):
        return pl.ds(pl.multiple_of(peer * depth, 16), depth)

    def start_weights(l):
        ref = refs.weights.at[l]
        cols = pl.ds(0, out_at), pl.ds(out_at, inner)
        return [start_shared(lambda i, c=c: ref.at[depth_block(i), c]) for c in cols]

    params = refs.params
    heads = refs.dt_bias.shape[1]
    eye_i = lax.broadcasted_iota(jnp.int32, (depth, depth), 0)
    eye_j = lax.broadcasted_iota(jnp.int32, (depth, depth), 1)
    eye = (eye_i == eye_j).astype(F32).astype(BF16)
    for l in range(layers):
        params[l] = jnp.zeros_like(params[l])
        params[l, 0:4, :inner] = refs.conv_x[l]
        params[l, 0:4, inner:conv_width] = refs.conv_bc[l]
        params[l, 4:5, :inner] = refs.conv_x_bias[l : l + 1, :]
        params[l, 4:5, inner:conv_width] = refs.conv_bc_bias[l : l + 1, :]
        params[l, 5:6, :inner] = refs.gate_gain[l : l + 1, :]
        params[l, 6:7, :] = refs.norm_gain[l : l + 1, :]
        params[l, 7:8, :heads] = refs.dt_bias[l : l + 1, :]
        params[l, 8:9, :heads] = refs.a_log[l : l + 1, :]
        params[l, 10:11, :heads] = refs.d_skip[l : l + 1, :]
        params[l, 8:16, :inner] = jnp.where(
            lax.broadcasted_iota(jnp.int32, (8, inner), 0) == 1,
            pltpu.roll(fine_dot(params[l, 8:16, :LANES], spread[...]), 7, 0),
            params[l, 8:16, :inner],
        )
        if gather_weights:
            W = refs.weights.at[l]
            mine = depth_block(a)
            W[mine, :inner] = refs.w_zx[l, :, 0, :]
            W[mine, inner:bc_at] = refs.w_zx[l, :, 1, :]
            W[mine, bc_at:dt_at] = refs.w_bc[l]
            W[mine, dt_at:out_at] = jnp.zeros((depth, LANES), BF16)
            W[mine, dt_at : dt_at + heads] = dot(eye, refs.w_dt[:, l, :], 1, 1).astype(BF16)
            W[mine, out_at:] = refs.w_out[l]

    own_x = own_rows(refs.x_all, HALO)
    own_x[...] = refs.x_in[...]
    own_c = own_rows(refs.cot_all)
    own_c[...] = refs.cotangent[...]

    pl.semaphore_wait(barrier, greeted)

    seg_base = lx.take()
    seg_copy = lx.copy(
        seg_ext.at[pl.ds(T, HALO)],
        seg_ext.at[pl.ds(0, HALO)],
        {DP: following, TP: t},
        seg_base,
        seg_base,
    )
    seg_copy.start()
    rows_done = start_rows(refs.x_all, HALO, True)
    nothing = [lambda: None] * 2
    weights_done = start_weights(0) if gather_weights else nothing
    seg_copy.wait()
    seg_ext[0:HALO, :] = jnp.where(a == 0, -1.0, seg_ext[0:HALO, :])
    for k in range(3):
        masks[k] = (seg_ext[pl.ds(HALO - 3 + k, T), :] == seg_col).astype(F32)
    first_seg, last_seg = seg_ext[HALO : HALO + 1, :], seg_ext[ext_rows - 1 :, :]
    reached = (seg_col == first_seg).astype(F32)
    kept = (seg_col == last_seg).astype(F32)
    joined = wide((seg_ext[HALO - 1 : HALO, :] == first_seg).astype(F32), chunks)
    whole_seg = wide((last_seg == first_seg).astype(F32), chunks)
    refs.reached[...] = reached
    refs.kept[...] = kept
    rows_done()

    def row(l, at, width):
        return refs.params[l, at : at + 1, :width]

    def norm_rows(h, gain):
        scale = lax.rsqrt(jnp.mean(h * h, axis=1, keepdims=True) + EPSILON)
        return (h * scale * gain).astype(BF16)

    refs.normed[0] = norm_rows(refs.x_all[...].astype(F32), row(0, 6, D))
    refs.hidden[0] = own_x[...].astype(F32)

    def as_column(value):
        return fine_dot(value, jnp.full((8, LANES), 0.125, BF16), 0, 0)

    def row_sums(value):
        return fine_dot_rows(value)

    def fine_dot_rows(value):
        ones = jnp.ones((8, inner), BF16)
        return sum(dot(ones, part, 1, 1) for part in pieces(value, 2))

    def forward(l):
        W = refs.weights.at[l]
        nx, ext, pre, act = (r.at[l] for r in (refs.normed, refs.ext, refs.pre, refs.act))
        tokens = pl.ds(HALO, T)
        ext[...] = dot(nx[...], W[:, inner:dt_at]).astype(BF16).astype(F32)
        dtb = dot(nx[tokens, :], W[:, dt_at:out_at]) + row(l, 7, LANES)
        for c in range(conv_width // LANES):
            at = slice(c * LANES, (c + 1) * LANES)
            taps = refs.params[l, 0:5, at]
            total = taps[4:5] + taps[3:4] * ext[tokens, at]
            for k in range(3):
                total = total + taps[k : k + 1] * ext[pl.ds(HALO - 3 + k, T), at] * masks[k]
            pre[:, at] = total
            act[:, at] = total * sigmoid(total)
        step = jnp.maximum(dtb, 0.0) + jnp.log1p(jnp.exp(-jnp.abs(dtb)))
        decay = -step * jnp.exp(row(l, 8, LANES))
        cum = sum(dot(below[...], part) for part in pieces(decay, 3))
        refs.dtb[l] = dtb
        refs.decay[l] = decay
        step_wide = fine_dot(step, spread[...])
        cum_wide = fine_dot(cum, spread[...])
        end = cum_wide[T - 1 :, :]
        from_start = jnp.exp(cum_wide) * wide(refs.reached[...], chunks)
        to_end = jnp.exp(end - cum_wide) * wide(refs.kept[...], chunks)
        refs.step_wide[l] = step_wide
        refs.from_start[l] = from_start
        refs.to_end[l] = to_end
        end_decay = jnp.exp(end)
        refs.end_decay[l] = end_decay
        xs = act[:, :inner]
        scaled = xs * step_wide
        refs.scaled[l] = scaled.astype(BF16)
        bmat = act[:, inner : inner + state_width].astype(BF16)
        cmat = act[:, inner + state_width :].astype(BF16)
        refs.bmat[l] = bmat
        refs.cmat[l] = cmat
        states, coefs = refs.states.at[l], refs.coefs.at[l]
        states[a, :state_width] = dot(bmat, (scaled * to_end).astype(BF16), 0, 0).astype(BF16)
        parts = pieces(joined * whole_seg * end_decay, 3)
        states[a, state_width:] = jnp.concatenate(
            parts + [jnp.zeros((13, inner), BF16)], axis=0
        )
        states_done = start_shared(lambda i: states.at[i])
        refs.z[l] = dot(nx[tokens, :], W[:, :inner])
        scores = dot(cmat, bmat, 1, 1)
        cum_rows = cum.T
        for c in range(chunks):
            at = slice(c * LANES, (c + 1) * LANES)
            pair = refs.scaled[l, :, at]
            found = []
            for u in range(per):
                h = c * per + u
                span = cum[:, h : h + 1] - cum_rows[h : h + 1, :] + bias[...]
                kernel_h = jnp.exp(span)
                refs.spans[l, h] = kernel_h
                mixed_h = (kernel_h * scores).astype(BF16)
                refs.mixing[l, h] = mixed_h
                found.append(dot(mixed_h, pair))
            refs.ssd[l, :, at] = choose(found) + row(l, 9, inner)[:, at] * act[:, at]
        states_done()

        def keep(s, carry):
            coefs[s] = jnp.broadcast_to(
                jnp.sum(states[s, state_width:].astype(F32), axis=0, keepdims=True), (8, inner)
            )
            return carry

        lax.fori_loop(0, dc, keep, 0)
        return states, coefs

    def choose(found):
        result = found[0]
        for u in range(1, per):
            result = jnp.where(lane < u * head_width, result, found[u])
        return result

    def enter(values, coefs, backward):
        def step(i, state):
            s = dc - 1 - i if backward else i
            ahead = s > a if backward else s < a
            later = values[s, :state_width].astype(F32) + coefs[s][0:1, :] * state
            return jnp.where(ahead, later, state)

        return lax.fori_loop(0, dc, step, jnp.zeros((state_width, inner), F32))

    def gate(l, states, coefs):
        start = joined * enter(states, coefs, False)
        refs.start[l] = start
        refs.ssd[l] = refs.ssd[l] + refs.from_start[l] * dot(
            refs.cmat[l], start.astype(BF16)
        )
        z = refs.z[l]
        return refs.ssd[l] * (z * sigmoid(z))

    def project_out(l, gated, parts):
        W = refs.weights.at[l]
        unscaled = (gated * row(l, 5, inner)).astype(BF16)
        refs.partial[l] = dot(unscaled, W[:, out_at:], 1, 1).astype(BF16)
        return start_sums(refs.partial.at[l], 0, refs.landed.at[l], parts)

    def summed_rows(ref, count, rows):
        total = ref[0, rows].astype(F32)
        for s in range(1, count):
            total = total + ref[s, rows].astype(F32)
        return total

    def summed(ref, count):
        total = ref[0].astype(F32)
        for s in range(1, count):
            total = total + ref[s].astype(F32)
        return total

    def inverse_from(l):
        squares = summed(refs.tokens.at[l], tc)
        inverse = lax.rsqrt(squares[0:8] / full_inner + EPSILON)
        refs.inverse[l] = as_column(inverse)
        return squares

    own_tokens = pl.ds(pl.multiple_of(t * R, 16), R)

    cot_done = start_rows(refs.cot_all, 0, False)
    weights_done[0]()
    states, coefs = forward(0)
    weights_done[1]()
    weights_done = start_weights(1) if gather_weights else nothing
    gated = gate(0, states, coefs)
    refs.tokens[0, t] = jnp.concatenate([fine_dot_rows(gated * gated)] * 2, axis=0)
    squares_done = start_blocks(refs.tokens.at[0], TP)
    branch_done = project_out(0, gated, steps)
    squares_done()
    inverse_from(0)
    rows_done = []
    for part in range(steps):
        branch_done(part)
        rows = pl.ds(part * n, n)
        tokens = pl.ds(pl.multiple_of(t * R + part * n, 16), n)
        branch = summed_rows(refs.landed.at[0], tc, rows)
        refs.unscaled[rows, :] = branch
        h1 = refs.hidden[0, rows] + wide(refs.inverse[0, tokens, :], D // LANES) * branch
        refs.hidden[1, rows] = h1
        own_n = part_rows(refs.normed.at[1], HALO, part, steps)
        own_n[...] = norm_rows(h1, row(1, 6, D))
        rows_done.append(start_rows(refs.normed.at[1], HALO, part == steps - 1, part, steps))
    cot_done()
    for done in weights_done:
        done()
    for done in rows_done:
        done()
    states, coefs = forward(1)
    W1 = refs.weights.at[1]
    d_mixed = dot(refs.cot_all[...], W1[:, out_at:])
    gated = gate(1, states, coefs)
    refs.tokens[1, t] = jnp.concatenate(
        [fine_dot_rows(gated * gated), fine_dot_rows(d_mixed * gated * row(1, 5, inner))], axis=0
    )
    squares_done = start_blocks(refs.tokens.at[1], TP)
    out_done = project_out(1, gated, 1)
    squares_done()
    totals = inverse_from(1)
    inner_dot = as_column(totals[8:16])

    def head_sums(value, count=2):
        return sum(dot(part, spread[...], 1, 1) for part in pieces(value, count))

    def put_small(l, at, value, lane_at=0):
        refs.small[l, at : at + value.shape[0], lane_at : lane_at + value.shape[1]] = value

    def column_sum(value):
        return jnp.sum(value, axis=0, keepdims=True)

    def backward(l, grad_rows, d_mixed, inner_dot):
        W = refs.weights.at[l]
        nx, ext, pre, act = (r.at[l] for r in (refs.normed, refs.ext, refs.pre, refs.act))
        d_all, d_low = refs.d_all, refs.d_low
        z, ssd = refs.z[l], refs.ssd[l]
        sig = sigmoid(z)
        silu = z * sig
        gated = ssd * silu
        inverse = wide(refs.inverse[l], chunks)
        gain = row(l, 5, inner)
        scaled_gate = gated * inverse
        d_gated = inverse * gain * d_mixed - scaled_gate * inverse * inverse * (
            wide(inner_dot, chunks) / full_inner
        )
        tokens = pl.ds(HALO, T)
        d_ssd = d_gated * silu
        d_ssd_low = d_ssd.astype(BF16)
        refs.d_ssd[...] = d_ssd_low
        from_start = (d_ssd * refs.from_start[l]).astype(BF16)
        d_states = refs.states.at[layers - 1 - l]
        cmat, bmat = refs.cmat[l], refs.bmat[l]
        d_states[a, :state_width] = (joined * dot(cmat, from_start, 0, 0)).astype(BF16)
        d_states_done = start_shared(lambda i: d_states.at[i, pl.ds(0, state_width)])
        mixed = (scaled_gate * gain).astype(BF16)
        put_small(l, 5, column_sum(d_mixed * scaled_gate))
        d_all[0:HALO, 0:inner] = jnp.zeros((HALO, inner), BF16)
        d_all[0:HALO, dt_at:out_at] = jnp.zeros((HALO, LANES), BF16)
        d_all[tokens, 0:inner] = (d_gated * ssd * sig * (1.0 + z * (1.0 - sig))).astype(BF16)
        start = refs.start[l]
        d_scores = jnp.zeros((T, T), F32)
        for c in range(chunks):
            at = slice(c * LANES, (c + 1) * LANES)
            pair, d_pair = refs.scaled[l, :, at], refs.d_ssd[:, at]
            found = []
            for u in range(per):
                h = c * per + u
                here = (lane >= u * head_width) & (lane < (u + 1) * head_width)
                d_mixing = dot(jnp.where(here, d_pair, jnp.zeros_like(d_pair)), pair, 1, 1)
                d_scores = d_scores + d_mixing * refs.spans[l, h]
                found.append(dot(refs.mixing[l, h], d_pair, 0, 0))
            refs.d_scaled[:, at] = choose(found)
        d_scores = d_scores.astype(BF16)
        d_cmat = dot(d_scores, bmat) + dot(from_start, start.astype(BF16), 1, 1)
        d_bmat = dot(d_scores, cmat, 0, 0)
        d_first, d_second = refs.d_first.at[l], refs.d_second.at[l]
        d_first[:, :inner] = dot(nx[...], d_all[:, :inner], 0, 0).astype(BF16)
        d_first[:, inner:] = dot(grad_rows, mixed, 0, 0).astype(BF16)
        d_states_done()
        if gather_weights:
            second = start_pairs(d_first, refs.pairs.at[l, 0], refs.got.at[l, 0])
        d_end = enter(d_states, refs.coefs.at[l], True)
        d_end_low = d_end.astype(BF16)
        to_end = refs.to_end[l]
        scaled_low = refs.scaled[l].astype(F32)
        from_end = to_end * dot(bmat, d_end_low)
        d_scaled = refs.d_scaled[...] + from_end
        d_bmat = d_bmat + dot((scaled_low * to_end).astype(BF16), d_end_low, 1, 1)
        xs = act[:, :inner]
        skip = row(l, 9, inner)
        d_cum = d_ssd_low.astype(F32) * (ssd - skip * xs) - scaled_low * d_scaled
        d_last = column_sum(scaled_low * from_end) + whole_seg * refs.end_decay[
            l
        ] * column_sum(d_end * start)
        is_last = lax.broadcasted_iota(jnp.int32, (T, inner), 0) == T - 1
        d_cum = head_sums(d_cum + jnp.where(is_last, d_last, 0.0), 3)
        d_decay = sum(dot(below[...], part, 0, 0) for part in pieces(d_cum, 3))
        d_step = head_sums(xs * d_scaled) - d_decay * jnp.exp(row(l, 8, LANES))
        d_dt = d_step * sigmoid(refs.dtb[l])
        d_all[tokens, dt_at:out_at] = d_dt.astype(BF16)
        put_small(l, 0, column_sum(d_dt), conv_width)
        put_small(l, 1, column_sum(d_decay * refs.decay[l]), conv_width)
        put_small(l, 2, head_sums(jnp.broadcast_to(column_sum(xs * d_ssd), (8, inner)))[0:1], conv_width)
        d_xs = refs.step_wide[l] * d_scaled + skip * d_ssd
        for c in range(conv_width // LANES):
            at = slice(c * LANES, (c + 1) * LANES)
            if c < chunks:
                d_act = d_xs[:, at]
            else:
                both = jnp.concatenate([d_bmat, d_cmat], axis=1)
                d_act = both[:, (c - chunks) * LANES : (c - chunks + 1) * LANES]
            p = pre[:, at]
            s = sigmoid(p)
            d_pre = d_act * s * (1.0 + p * (1.0 - s))
            taps = refs.params[l, 0:5, at]
            top = jnp.zeros((HALO, LANES), F32)
            refs.d_pre[:, at] = d_pre
            d_ext = jnp.concatenate([top, d_pre * taps[3:4]], axis=0)
            for k in range(3):
                moved = jnp.concatenate([top, d_pre * masks[k] * taps[k : k + 1]], axis=0)
                d_ext = d_ext + pltpu.roll(moved, ext_rows - 3 + k, 0)
            at_all = slice(inner + c * LANES, inner + (c + 1) * LANES)
            high = d_ext.astype(BF16)
            d_all[:, at_all] = high
            if c >= chunks:
                d_low[:, (c - chunks) * LANES : (c - chunks + 1) * LANES] = (
                    d_ext - high.astype(F32)
                ).astype(BF16)
        rows = dot(d_all[...], W[:, :out_at], 1, 1) + dot(d_low[...], W[:, bc_at:dt_at], 1, 1)
        refs.d_rows[l] = rows.astype(BF16)
        done = start_sums(refs.d_rows.at[l], HALO, refs.d_landed.at[l], steps)
        base = lx.take(tc + 1)

        def head_copy():
            return lx.copy(
                refs.d_rows.at[l].at[pl.ds(0, HALO)],
                refs.d_heads.at[l].at[t],
                {DP: prev, TP: jnp.int32(last_t)},
                base + tc,
                base + t,
            )

        head_copy().start()

        if gather_weights:
            first_done = second()
        maps = pl.ds(0, 2 * state_width)
        d_second[:, maps] = (
            dot(nx[...], d_all[:, bc_at:dt_at], 0, 0) + dot(nx[...], d_low[...], 0, 0)
        ).astype(BF16)
        d_second[:, 2 * state_width : inner] = dot(nx[...], d_all[:, dt_at:out_at], 0, 0).astype(
            BF16
        )
        halves = [pl.ds(0, inner), pl.ds(inner, inner)]

        def tap_sums():
            for c in range(conv_width // LANES):
                at = slice(c * LANES, (c + 1) * LANES)
                d_pre = refs.d_pre[:, at]
                put_small(l, 4, column_sum(d_pre), c * LANES)
                put_small(l, 3, column_sum(d_pre * ext[tokens, at]), c * LANES)
                for k in range(3):
                    part = d_pre * masks[k] * ext[pl.ds(HALO - 3 + k, T), at]
                    put_small(l, k, column_sum(part), c * LANES)

        def start_second(cols):
            return start_pairs(
                d_second.at[:, cols], refs.pairs.at[l, 1, :, :, cols], refs.got.at[l, 1, :, :, cols]
            )

        if gather_weights:
            second = start_second(halves[0])
        d_second[:, inner:] = dot(nx[...], d_all[:, inner:bc_at], 0, 0).astype(BF16)
        if gather_weights:
            maps_done = second()
            second = start_second(halves[1])
            second_done = second()
        tap_sums()

        def gradients():
            maps_done()
            refs.maps[l, t] = summed(refs.got.at[l, 1, :, :, maps], half).astype(BF16)
            maps_sent = start_blocks(refs.maps.at[l], TP)
            first_done()
            put_out(l, 0, summed(refs.got.at[l, 0], half))
            second_done()
            put_out(l, 1, summed(refs.got.at[l, 1], half))

            def last():
                maps_sent()
                put_maps(l, summed(refs.maps.at[l], tc))

            return last

        def finish(part):
            done(part)
            rows = pl.ds(part * n, n)
            refs.d_own[rows, :] = summed_rows(refs.d_landed.at[l], tc, rows)
            if part < steps - 1:
                return
            head_copy().wait_send()

            @pl.when(t == last_t)
            def _():
                for u in range(tc):
                    lx.copy(
                        refs.d_rows.at[l].at[pl.ds(0, HALO)],
                        refs.d_heads.at[l].at[u],
                        {DP: prev, TP: jnp.int32(last_t)},
                        base + tc,
                        base + u,
                    ).wait_recv()
                refs.d_own[R - HALO :, :] = refs.d_own[R - HALO :, :] + summed(
                    refs.d_heads.at[l], tc
                )

        return finish, gradients

    results = refs.results
    small_at, grads_at = 2 * R, 2 * R + layers * tc * 8

    def put_out(l, part, value):
        at = grads_at + (2 * l + part) * depth
        results[at : at + depth, :] = value

    def put_maps(l, value):
        at = grads_at + (2 * l + 1) * depth
        results[at : at + depth, 0 : 2 * state_width] = value

    def norm_back(l, grad, rows):
        h, d = refs.hidden[l, rows], refs.d_own[rows, :]
        scale = lax.rsqrt(jnp.mean(h * h, axis=1, keepdims=True) + EPSILON)
        refs.small[l, 6:7, :] = refs.small[l, 6:7, :] + column_sum(d * h * scale)
        weighted = d * row(l, 6, D)
        return (
            grad
            + scale * weighted
            - h * scale * scale * scale * jnp.mean(weighted * h, axis=1, keepdims=True)
        )

    for l in range(layers):
        refs.small[l] = jnp.zeros_like(refs.small[l])

    def start_small(l):
        refs.small_all[l, a] = refs.small[l]
        return start_blocks(refs.small_all.at[l], DP)

    finish, gradients1 = backward(1, refs.cot_all[...], d_mixed, inner_dot)
    grads_all = refs.grads_all
    grads_done = []
    for part in range(steps):
        finish(part)
        rows = pl.ds(part * n, n)
        first = part_rows(refs.cot_all, 0, part, steps)
        grad = norm_back(1, first[...].astype(F32), rows)
        refs.grad[rows, :] = grad
        low = grad.astype(BF16)
        here = part_rows(grads_all, 0, part, steps)
        here[:, :D] = low
        dots = jnp.sum(low.astype(F32) * refs.unscaled[rows, :], axis=1, keepdims=True)
        high, mid, rest = pieces(jnp.broadcast_to(dots, (n, LANES)), 3)
        zero = jnp.zeros_like(high)
        here[:, D:] = jnp.where(
            lane == 0, high, jnp.where(lane == 1, mid, jnp.where(lane == 2, rest, zero))
        )
        grads_done.append(start_rows(grads_all, 0, False, part, steps))
    small1 = start_small(1)
    out_done(0)
    results[0:R, :] = (
        refs.hidden[1]
        + wide(refs.inverse[1, own_tokens, :], D // LANES) * summed(refs.landed.at[1], tc)
    )
    for done in grads_done:
        done()
    d_mixed = dot(grads_all[:, :D], refs.weights[0, :, out_at:])
    inner_dot = jnp.broadcast_to(
        jnp.sum(grads_all[:, D:].astype(F32), axis=1, keepdims=True), (T, LANES)
    )
    finish, gradients0 = backward(0, grads_all[:, :D], d_mixed, inner_dot)
    if gather_weights:
        last1 = gradients1()
    for part in range(steps):
        finish(part)
        rows = pl.ds(part * n, n)
        results[R + part * n : R + part * n + n, :] = norm_back(0, refs.grad[rows, :], rows)
    small0 = start_small(0)
    small1()
    refs.small_out[1, t] = summed(refs.small_all.at[1], dc)
    sent1 = start_blocks(refs.small_out.at[1], TP)
    small0()
    refs.small_out[0, t] = summed(refs.small_all.at[0], dc)
    sent0 = start_blocks(refs.small_out.at[0], TP)
    if gather_weights:
        last0 = gradients0()
        last1()
        last0()
    sent1()
    sent0()
    for l in range(layers):
        for u in range(tc):
            at = small_at + (l * tc + u) * 8
            results[at : at + 8, :] = refs.small_out[l, u]
    return lx.used


def local(
    x_in,
    segment_ids,
    norm_gain,
    w_zx,
    w_dt,
    w_bc,
    conv_x,
    conv_x_bias,
    conv_bc,
    conv_bc_bias,
    dt_bias,
    a_log,
    d_skip,
    gate_gain,
    w_out,
    cotangent,
):
    layers, D = norm_gain.shape
    tc, dc = lax.axis_size(TP), lax.axis_size(DP)
    R = x_in.shape[0]
    T = segment_ids.shape[0]
    inner = conv_x.shape[2]
    heads = dt_bias.shape[1]
    state_pair = w_bc.shape[2]
    state_width = state_pair // 2
    head_width = inner // heads
    conv_width = inner + state_pair
    dt_at = inner + conv_width
    out_at = dt_at + LANES
    columns = out_at + inner
    depth = w_bc.shape[1]
    gather_weights = depth % 16 == 0
    bc_at = 2 * inner

    ins = dict(
        x_in=x_in,
        cotangent=cotangent,
        segs=segment_ids.reshape(1, T),
        norm_gain=norm_gain,
        conv_x=conv_x,
        conv_x_bias=conv_x_bias,
        conv_bc=conv_bc,
        conv_bc_bias=conv_bc_bias,
        dt_bias=dt_bias,
        a_log=a_log,
        d_skip=d_skip,
        gate_gain=gate_gain,
    )
    if gather_weights:
        ins.update(
            w_zx=w_zx,
            w_bc=w_bc,
            w_dt=jnp.transpose(w_dt, (2, 0, 1)),
            w_out=jnp.swapaxes(w_out, 1, 2),
        )
    else:
        packed = jnp.concatenate(
            [
                w_zx.reshape(layers, depth, bc_at),
                w_bc,
                jnp.pad(w_dt, ((0, 0), (0, 0), (0, LANES - heads))),
                jnp.swapaxes(w_out, 1, 2),
            ],
            axis=2,
        )
        ins.update(weights=lax.all_gather(packed, DP, axis=1, tiled=True))

    ext_rows = T + HALO
    S = jax.ShapeDtypeStruct
    grads_rows = layers * 2 * depth if gather_weights else 0
    outs = dict(results=S((2 * R + layers * tc * 8 + grads_rows, D), F32))
    if not gather_weights:
        outs.update(d_first=S((layers, D, D), BF16), d_second=S((layers, D, D), BF16))
    scratch = dict(
        spread=((LANES, inner), BF16),
        params=((layers, 16, D), F32),
        below=((T, T), BF16),
        seg_ext=((ext_rows, LANES), F32),
        masks=((3, T, LANES), F32),
        bias=((T, T), F32),
        reached=((T, LANES), F32),
        kept=((T, LANES), F32),
        x_all=((ext_rows, D), BF16),
        cot_all=((T, D), BF16),
        normed=((layers, ext_rows, D), BF16),
        hidden=((layers, R, D), F32),
        ext=((layers, ext_rows, conv_width), F32),
        pre=((layers, T, conv_width), F32),
        act=((layers, T, conv_width), F32),
        z=((layers, T, inner), F32),
        dtb=((layers, T, LANES), F32),
        decay=((layers, T, LANES), F32),
        step_wide=((layers, T, inner), F32),
        from_start=((layers, T, inner), F32),
        to_end=((layers, T, inner), F32),
        end_decay=((layers, 1, inner), F32),
        scaled=((layers, T, inner), BF16),
        bmat=((layers, T, state_width), BF16),
        cmat=((layers, T, state_width), BF16),
        states=((layers, dc, state_width + HALO, inner), BF16),
        coefs=((layers, dc, 8, inner), F32),
        spans=((layers, heads, T, T), F32),
        mixing=((layers, heads, T, T), BF16),
        ssd=((layers, T, inner), F32),
        d_pre=((T, conv_width), F32),
        start=((layers, state_width, inner), F32),
        partial=((layers, T, D), BF16),
        landed=((layers, tc, R, D), BF16),
        tokens=((layers, tc, 16, T), F32),
        inverse=((layers, T, LANES), F32),
        unscaled=((R, D), F32),
        d_all=((ext_rows, out_at), BF16),
        d_low=((ext_rows, state_pair), BF16),
        d_ssd=((T, inner), BF16),
        d_scaled=((T, inner), F32),
        d_rows=((layers, ext_rows, D), BF16),
        d_landed=((layers, tc, R, D), BF16),
        d_heads=((layers, tc, HALO, D), BF16),
        d_own=((R, D), F32),
        grad=((R, D), F32),
        grads_all=((T, D + LANES), BF16),
        small=((layers, 8, D), F32),
        small_out=((layers, tc, 8, D), F32),
        small_all=((layers, dc, 8, D), F32),
    )
    if gather_weights:
        scratch.update(
            weights=((layers, D, columns), BF16),
            d_first=((layers, D, columns // 2), BF16),
            d_second=((layers, D, columns // 2), BF16),
            pairs=((layers, 2, dc // 2, depth, columns // 2), BF16),
            got=((layers, 2, dc // 2, depth, columns // 2), BF16),
            maps=((layers, tc, depth, state_pair), BF16),
        )
    names = list(ins) + list(outs) + list(scratch) + ["send", "recv"]
    sizes = (layers, T, D, inner, conv_width, dc, tc, gather_weights, state_width)
    semaphores = 20 * dc + 40 * tc if gather_weights else 8 * dc + 40 * tc

    def kernel(*args):
        refs = types.SimpleNamespace(**dict(zip(names, args)))
        refs.head_width = head_width
        used = whole_step(sizes, refs)
        assert used <= semaphores, used

    vmem = pl.BlockSpec(memory_space=pltpu.VMEM)
    results = pl.pallas_call(
        kernel,
        out_shape=tuple(outs.values()),
        in_specs=[vmem] * len(ins),
        out_specs=tuple([vmem] * len(outs)),
        scratch_shapes=[pltpu.VMEM(shape, kind) for shape, kind in scratch.values()]
        + [pltpu.SemaphoreType.DMA((semaphores,))] * 2,
        compiler_params=pltpu.CompilerParams(
            collective_id=1, has_side_effects=True, vmem_limit_bytes=60 * 1024 * 1024
        ),
    )(*ins.values())
    found = dict(zip(outs, results))
    small_at, grads_at = 2 * R, 2 * R + layers * tc * 8
    room_of = depth + -depth % 8
    all_results = found["results"]
    if not gather_weights:
        d_out = jnp.stack(
            [
                lax.psum_scatter(found[n].astype(F32), DP, scatter_dimension=1, tiled=True)
                for n in ("d_first", "d_second")
            ],
            axis=1,
        )
        d_maps = lax.psum(d_out[:, 1, :, :state_pair], TP)
        d_out = d_out.at[:, 1, :, :state_pair].set(d_maps)
        fill = (0, room_of - depth)
        d_out = jnp.pad(d_out, ((0, 0), (0, 0), fill, (0, 0))).reshape(-1, D)
        all_results = jnp.concatenate([all_results, d_out], axis=0)
    lasts = (
        S((R, D), BF16),
        S((R, D), F32),
        S((layers, D), F32),
        S((layers, depth, 2, inner), F32),
        S((heads, layers, depth), F32),
        S((layers, depth, state_pair), F32),
        S((layers, conv_x.shape[1], tc * inner), F32),
        S((layers, tc * inner), F32),
        S(conv_bc.shape, F32),
        S(conv_bc_bias.shape, F32),
        S((layers, tc * heads), F32),
        S((layers, tc * heads), F32),
        S((layers, tc * heads), F32),
        S((layers, tc * inner), F32),
        S((layers, depth, inner), F32),
    )

    def unpack(found, *refs):
        y, dx, dgain, dzx, ddt, dbc, dcx, dcxb, dcb, dcbb, ddtb, dal, dsk, dgate, dwo, room = refs
        y[...] = found[0:R, :].astype(BF16)
        dx[...] = found[R : 2 * R, :]
        taps = conv_x.shape[1]
        for l in range(layers):
            at = slice(l, l + 1)
            small = [found.at[pl.ds(small_at + (l * tc + u) * 8, 8)] for u in range(tc)]
            first = pl.ds(grads_at + 2 * l * room_of, depth)
            second = pl.ds(grads_at + (2 * l + 1) * room_of, depth)
            dgain[at, :] = sum(small[u][6:7, :] for u in range(tc))
            dcb[l] = sum(small[u][0:taps, inner:conv_width] for u in range(tc))
            dcbb[at, :] = sum(small[u][4:5, inner:conv_width] for u in range(tc))
            rows = jnp.zeros((8, LANES), F32)
            for u in range(tc):
                cols = slice(u * inner, (u + 1) * inner)
                dcx[l, :, cols] = small[u][0:taps, :inner]
                dcxb[at, cols] = small[u][4:5, :inner]
                dgate[at, cols] = small[u][5:6, :inner]
                rows = rows + pltpu.roll(small[u][:, conv_width:], u * heads, 1)
            ddtb[at, :] = rows[0:1, : tc * heads]
            dal[at, :] = rows[1:2, : tc * heads]
            dsk[at, :] = rows[2:3, : tc * heads]
            dbc[l] = found[second, :state_pair]
            room[0:depth, :] = found[second, state_pair:inner]
            ddt[:, l, :] = room[...].T[:heads, :depth]
            dzx[l, :, 0, :] = found[first, :inner]
            dzx[l, :, 1, :] = found[second, inner:]
            dwo[l] = found[first, inner:]

    last = pl.pallas_call(
        unpack,
        out_shape=lasts,
        in_specs=[vmem],
        out_specs=tuple([vmem] * len(lasts)),
        scratch_shapes=[pltpu.VMEM((LANES, LANES), F32)],
        compiler_params=pltpu.CompilerParams(vmem_limit_bytes=32 * 1024 * 1024),
    )(all_results)
    return last[:4] + (jnp.transpose(last[4], (1, 2, 0)),) + last[5:14] + (jnp.swapaxes(last[14], 1, 2),)


def solution(mesh):
    return jax.shard_map(
        local,
        mesh=mesh,
        in_specs=(
            P((DP, TP), None),
            P(DP),
            P(),
            P(None, DP, None, TP),
            P(None, DP, TP),
            P(None, DP, None),
            P(None, None, TP),
            P(None, TP),
            P(),
            P(),
            P(None, TP),
            P(None, TP),
            P(None, TP),
            P(None, TP),
            P(None, TP, DP),
            P((DP, TP), None),
        ),
        out_specs=(
            P((DP, TP), None),
            P((DP, TP), None),
            P(),
            P(None, DP, None, TP),
            P(None, DP, TP),
            P(None, DP, None),
            P(),
            P(),
            P(),
            P(),
            P(),
            P(),
            P(),
            P(),
            P(None, TP, DP),
        ),
        check_vma=False,
    )
```
